32 devices in a mesh: slab: 2 (over x), shot: 8 (over z, y), rcv: 2 (over core).
Axes of the slice: x: 2, y: 2, z: 4, core: 2. Of those that a mesh axis runs over, the one named last changes fastest.
Arguments:
- traces: bfloat16 [16, 256, 1536], P(('slab', 'shot'), 'rcv'), parts along dimension 0, may hold values from -6 to 6
- rcv_delay: int32 [16, 256, 9], P(('slab', 'shot'), 'rcv'), parts along dimension 0, may hold values from 0 to 47
- rcv_frac: int32 [16, 256, 9], P(('slab', 'shot'), 'rcv'), parts along dimension 0, may hold values from 0 to 255
- live_count: int32 [16], P(('slab', 'shot')), parts along dimension 0, may hold values from 64 to 256
- src_delay: int32 [16, 2, 128, 9], P('slab', 'rcv', 'shot'), parts along dimension 0, may hold values from 0 to 47
- src_frac: int32 [16, 2, 128, 9], P('slab', 'rcv', 'shot'), parts along dimension 0, may hold values from 0 to 255
- rcv_taper: float32 [9], replicated, may hold values from 0.5 to 1.5
- src_taper: float32 [9], replicated, may hold values from 0.5 to 1.5
Outputs:
- redatumed: bfloat16 [16, 2, 128, 1536], P('slab', 'rcv', 'shot'), parts along dimension 0
The draws below stay inside these ranges and needn't reach their ends.
There are 2 independent parts, one for each index of `slab`. The reference program is written for one: setup_inputs(seed, part) draws one part's arguments, and reference() takes and returns one part's arrays. A program takes and returns all parts, laid end to end along the dimension named above; an argument that names none is the same for every part. Nothing has to cross between parts.
All inputs are finite; a program needn't handle non-finite values.
Results may differ from the reference program's by a relative error of at most 0.0055.
Values may be sent and summed in bfloat16 or wider, within the bound.
No kernel may reach another device: no remote copies, remote signals or barrier semaphores. Data moves between devices by JAX's collectives and lax.ppermute only.
A program may use at most 64 MiB of HBM per device.

```python
import jax
import jax.numpy as jnp

NT = 1536
NR = 256
AR = 4
AS = 4
TRI = 2
DMAX = 48
KR = 9
KS = 9
NS = 8
N_RCV = 2


def set_ends(drawn, key, low, high):
    longest = drawn.shape.index(max(drawn.shape))
    spots = []
    for shift in (0, 1):
        where = [jax.random.randint(jax.random.fold_in(key, axis), (), 0, length) for axis, length in enumerate(drawn.shape)]
        where[longest] = (where[longest] + shift) % drawn.shape[longest]
        spots.append(tuple(where))
    return drawn.at[spots[0]].set(low).at[spots[1]].set(high)


def shard_levels(key, extent, cuts, low, high):
    factor_of = 1.0
    for dim, shards_of in cuts:
        heights = jax.random.uniform(jax.random.fold_in(jax.random.fold_in(key, 6), dim), (shards_of,), jnp.float32, low / len(cuts), high / len(cuts))
        factor_of = factor_of * jnp.repeat(jnp.exp(heights), extent[dim] // shards_of).reshape((-1,) + (1,) * (len(extent) - 1 - dim))
    return factor_of


def normal_values(stream_key, extent, width, limit, cuts=(), held_as=jnp.bfloat16):
    level = shard_levels(stream_key, extent, cuts, -0.22, 0.18) if cuts else 1.0
    values = jax.random.normal(stream_key, extent, jnp.float32) * width * level
    return jnp.minimum(jnp.maximum(values, -limit), limit).astype(held_as)


def setup_inputs(seed: int = 0, part: int = 0) -> dict:
    keys = jax.random.split(jax.random.key(seed), 9)
    part_keys = jax.random.split(jax.random.fold_in(keys[8], part), 9)
    traces = normal_values(part_keys[0], (NS, NR, NT), 1.0, 6.0, ((0, 8), (1, 2)))
    rcv_delay = set_ends(jax.random.randint(part_keys[1], (NS, NR, KR), 0, DMAX), jax.random.fold_in(part_keys[1], 1), 0, DMAX - 1).astype(jnp.int32)
    rcv_frac = set_ends(jax.random.randint(part_keys[2], (NS, NR, KR), 0, 256), jax.random.fold_in(part_keys[2], 1), 0, 255).astype(jnp.int32)
    live_count = set_ends(jax.random.randint(part_keys[3], (NS,), NR // 4, NR + 1), jax.random.fold_in(part_keys[3], 1), NR // 4, NR).astype(jnp.int32)
    src_delay = set_ends(jax.random.randint(part_keys[4], (NS, N_RCV, NR // N_RCV, KS), 0, DMAX), jax.random.fold_in(part_keys[4], 1), 0, DMAX - 1).astype(jnp.int32)
    src_frac = set_ends(jax.random.randint(part_keys[5], (NS, N_RCV, NR // N_RCV, KS), 0, 256), jax.random.fold_in(part_keys[5], 1), 0, 255).astype(jnp.int32)
    rcv_taper = jnp.clip(jax.random.uniform(keys[6], (KR,), jnp.float32, 0.5, 1.5), 0.5, 1.5)
    src_taper = jnp.clip(jax.random.uniform(keys[7], (KS,), jnp.float32, 0.5, 1.5), 0.5, 1.5)
    return dict(traces=traces, rcv_delay=rcv_delay, rcv_frac=rcv_frac, live_count=live_count, src_delay=src_delay, src_frac=src_frac, rcv_taper=rcv_taper, src_taper=src_taper)


def triangle_matrix():
    rows = jnp.arange(NT, dtype=jnp.int32)[:, None]
    cols = jnp.arange(NT, dtype=jnp.int32)[None, :]
    height = jnp.maximum(TRI - jnp.abs(cols - rows), 0).astype(jnp.float32)
    energy = jnp.sum(jnp.maximum(TRI - jnp.abs(jnp.arange(-TRI, TRI + 1, dtype=jnp.int32)), 0).astype(jnp.float32) ** 2)
    return (height / jnp.sqrt(energy)).astype(jnp.bfloat16)

def apply_filter(block, matrix):
    flat = block.reshape(-1, NT)
    return jnp.dot(flat, matrix, preferred_element_type=jnp.float32).astype(jnp.bfloat16).reshape(block.shape)

def read_shifted(source, delay, frac):
    padded = jnp.pad(source, [(0, 0)] * (source.ndim - 1) + [(0, DMAX + 1)])
    index = jnp.arange(NT, dtype=jnp.int32) + delay[..., None].astype(jnp.int32)
    first = jnp.take_along_axis(padded, index, axis=-1).astype(jnp.float32)
    second = jnp.take_along_axis(padded, index + 1, axis=-1).astype(jnp.float32)
    weight = frac[..., None].astype(jnp.float32) / 256.0
    return (1.0 - weight) * first + weight * second

def reference(traces, rcv_delay, rcv_frac, live_count, src_delay, src_frac, rcv_taper, src_taper):
    matrix = triangle_matrix()
    filtered = apply_filter(traces, matrix)
    padded = jnp.pad(filtered, ((0, 0), (AR, AR), (0, 0)))
    total = jnp.zeros(traces.shape, jnp.float32)
    fold = jnp.zeros(traces.shape[:2], jnp.float32)
    for tap in range(KR):
        source = padded[:, tap:tap + NR, :]
        where = jnp.arange(NR, dtype=jnp.int32) + tap - AR
        live = ((where >= 0) & (where < NR))[None, :] & (where[None, :] < live_count[:, None])
        live = live.astype(jnp.float32)
        total = total + rcv_taper[tap] * live[..., None] * read_shifted(source, rcv_delay[:, :, tap], rcv_frac[:, :, tap])
        fold = fold + live
    section_one = (total / jnp.sqrt(jnp.maximum(fold, 1.0))[..., None]).astype(jnp.bfloat16)
    second = apply_filter(section_one, matrix)
    spaced = jnp.pad(second, ((AS, AS), (0, 0), (0, 0)))
    delay_two = src_delay.reshape(NS, NR, KS)
    frac_two = src_frac.reshape(NS, NR, KS)
    result = jnp.zeros(traces.shape, jnp.float32)
    count = jnp.zeros((NS,), jnp.float32)
    for tap in range(KS):
        source = spaced[tap:tap + NS]
        where = jnp.arange(NS, dtype=jnp.int32) + tap - AS
        inside = ((where >= 0) & (where < NS)).astype(jnp.float32)
        result = result + src_taper[tap] * inside[:, None, None] * read_shifted(source, delay_two[:, :, tap], frac_two[:, :, tap])
        count = count + inside
    result = result / jnp.sqrt(count)[:, None, None]
    return result.astype(jnp.bfloat16).reshape(NS, N_RCV, NR // N_RCV, NT)
```

```python
import functools
import math

import jax
import jax.numpy as jnp
from jax import lax
from jax.experimental import pallas as pl
from jax.experimental.pallas import tpu as pltpu
from jax.sharding import PartitionSpec as P

AR = 4
AS = 4
TRI = 2
KR = 9
KS = 9
LANES = 128
F32 = jnp.float32
BF16 = jnp.bfloat16


def filter_band():
    rows = lax.broadcasted_iota(jnp.int32, (3 * LANES, LANES), 0) - LANES
    cols = lax.broadcasted_iota(jnp.int32, (3 * LANES, LANES), 1)
    height = jnp.maximum(TRI - jnp.abs(cols - rows), 0).astype(F32)
    energy = float(sum((TRI - abs(m)) ** 2 for m in range(1 - TRI, TRI)))
    return (height / math.sqrt(energy)).astype(BF16)


def filtered_block(source, block, blocks, band):
    low, high = max(block - 1, 0), min(block + 2, blocks)
    part = source[:, low * LANES : high * LANES]
    start = (low - block + 1) * LANES
    dot = jnp.dot(part, band[start : start + (high - low) * LANES], preferred_element_type=F32)
    return dot.astype(BF16).astype(F32)


def add_tap(first, second, load, blocks, delay, frac, taper, lane):
    place = lane + delay
    index = place & (LANES - 1)
    here = place < LANES
    weight = frac.astype(F32) * (1.0 / 256.0)
    one = taper * (1.0 - weight)
    two = taper * weight
    moved = [jnp.take_along_axis(load(b), index, axis=1) for b in range(blocks)]
    moved.append(jnp.zeros_like(moved[0]))
    for b in range(blocks):
        value = jnp.where(here, moved[b], moved[b + 1])
        first[b] = first[b] + one * value
        second[b] = second[b] + two * value


def join(first, second, blocks, lane):
    rolled = [pltpu.roll(v, LANES - 1, 1) for v in second] + [jnp.zeros_like(second[0])]
    inner = lane < LANES - 1
    return [first[b] + jnp.where(inner, rolled[b], rolled[b + 1]) for b in range(blocks)]


def receiver_kernel(far, peers, live_ref, taper_ref, traces_ref, edge_ref, delay_ref, frac_ref, out_ref, src_ref):
    rows, time = traces_ref.shape
    blocks = time // LANES
    halves = 2
    part = rows // halves
    per_peer = rows // peers
    group = min(8, per_peer)
    me = lax.axis_index("shot")
    mine = me // (peers // 2)
    half = (1 - mine) if far else mine
    low = me % (peers // 2)
    block_of = lax.axis_index("rcv")
    groups = lax.axis_size("rcv")
    base = pl.multiple_of(half * part, part)
    edge = edge_ref.shape[0]

    left_in = traces_ref[pl.ds(pl.multiple_of(jnp.maximum(base - edge, 0), edge), edge), :]
    right_in = traces_ref[pl.ds(pl.multiple_of(jnp.minimum(base + part, rows - edge), edge), edge), :]
    other = edge_ref[...]
    left = jnp.where(half == 0, other, left_in)
    right = jnp.where(half == halves - 1, other, right_in)
    source = jnp.concatenate([left, traces_ref[pl.ds(base, part), :], right], axis=0)
    height = part + 2 * edge
    where = lax.broadcasted_iota(jnp.int32, (height, LANES), 0) + (block_of * rows + base - edge)
    live = live_ref[0]
    alive = (where >= 0) & (where < rows * groups) & (where < live)
    band = filter_band()
    for b in range(blocks):
        src_ref[b] = jnp.where(alive, filtered_block(source, b, blocks, band), 0.0)

    lane = lax.broadcasted_iota(jnp.int32, (8, LANES), 1)
    line = lax.broadcasted_iota(jnp.int32, (8, LANES), 0)
    last = jnp.minimum(live, rows * groups) - 1
    for g in range(part // 8):
        at = pl.ds(pl.multiple_of(base + g * 8, 8), 8)
        delay, frac = delay_ref[at, :], frac_ref[at, :]
        first = [jnp.zeros((8, LANES), F32) for _ in range(blocks)]
        second = [jnp.zeros((8, LANES), F32) for _ in range(blocks)]
        for a in range(KR):
            row = edge + g * 8 + a - AR
            add_tap(
                first,
                second,
                lambda b: src_ref[b, row : row + 8, :],
                blocks,
                jnp.broadcast_to(delay[:, a : a + 1], (8, LANES)),
                jnp.broadcast_to(frac[:, a : a + 1], (8, LANES)),
                taper_ref[a],
                lane,
            )
        here = line + (block_of * rows + base + g * 8)
        fold = jnp.minimum(here + AR, last) - jnp.maximum(here - AR, 0) + 1
        scale = 1.0 / jnp.sqrt(jnp.maximum(fold, 1).astype(F32))
        total = join(first, second, blocks, lane)
        for s in range(8 // group):
            row = g * 8 + s * group
            peer = (row // per_peer) ^ low
            for b in range(blocks):
                value = (total[b] * scale).astype(BF16)[s * group : (s + 1) * group]
                out_ref[peer, row % per_peer : row % per_peer + group, b * LANES : (b + 1) * LANES] = value


def receiver_side(far, peers, live, taper, traces, edge, delay, frac):
    rows, time = traces.shape
    vmem = pl.BlockSpec(memory_space=pltpu.VMEM)
    smem = pl.BlockSpec(memory_space=pltpu.SMEM)
    return pl.pallas_call(
        functools.partial(receiver_kernel, far, peers),
        out_shape=jax.ShapeDtypeStruct((peers // 2, rows // peers, time), BF16),
        in_specs=[smem, smem, vmem, vmem, vmem, vmem],
        out_specs=vmem,
        scratch_shapes=[pltpu.VMEM((time // LANES, rows // 2 + 2 * edge.shape[0], LANES), F32)],
        name="receiver_far" if far else "receiver_near",
    )(live, taper, traces, edge, delay, frac)


def source_kernel(far, peers, taper_ref, delay_ref, frac_ref, *refs):
    half_peers = peers // 2
    ins = refs[:half_peers]
    refs = refs[half_peers:]
    if far:
        part_ref, out_ref, src_ref = refs
    else:
        out_ref, src_ref = refs
    per_peer, time = ins[0].shape
    blocks = time // LANES
    me = lax.axis_index("shot")
    mine = me // half_peers
    half = (1 - mine) if far else mine
    low = me % half_peers
    flip = half == 1
    band = filter_band()
    for r in range(half_peers):
        near = low ^ r
        slot = jnp.where(flip, half_peers - 1 - near, near)
        source = ins[r][...]
        for b in range(blocks):
            src_ref[slot, b] = filtered_block(source, b, blocks, band)
    rows = min(8, per_peer)
    lane = lax.broadcasted_iota(jnp.int32, (rows, LANES), 1)
    for kk in range(peers):
        k = jnp.where(flip, peers - 1 - kk, kk)
        near = [pp for pp in range(half_peers) if abs(pp - kk) <= AS]
        count = min(kk + AS, peers - 1) - max(kk - AS, 0) + 1
        for i in range(per_peer // rows):
            at = slice(i * rows, (i + 1) * rows)
            first = [jnp.zeros((rows, LANES), F32) for _ in range(blocks)]
            second = [jnp.zeros((rows, LANES), F32) for _ in range(blocks)]
            delay, frac = delay_ref[k, at, :], frac_ref[k, at, :]
            flipped_d, flipped_f = delay, frac
            for pp in near:
                up, down = pp - kk + AS, kk - pp + AS
                dd = jnp.where(flip, delay[:, down : down + 1], delay[:, up : up + 1])
                ff = jnp.where(flip, frac[:, down : down + 1], frac[:, up : up + 1])
                add_tap(
                    first,
                    second,
                    lambda b: src_ref[pp, b, at, :],
                    blocks,
                    jnp.broadcast_to(dd, (rows, LANES)),
                    jnp.broadcast_to(ff, (rows, LANES)),
                    taper_ref[jnp.where(flip, down, up)],
                    lane,
                )
            total = join(first, second, blocks, lane) if near else first
            for b in range(blocks):
                cols = slice(b * LANES, (b + 1) * LANES)
                value = total[b]
                if far:
                    value = (value + part_ref[k, at, cols]) * (1.0 / math.sqrt(count))
                out_ref[k, at, cols] = value.astype(out_ref.dtype)


def source_side(far, peers, taper, delay, frac, ins, partial=None):
    per_peer, time = ins[0].shape
    vmem = pl.BlockSpec(memory_space=pltpu.VMEM)
    smem = pl.BlockSpec(memory_space=pltpu.SMEM)
    extra = [partial] if far else []
    return pl.pallas_call(
        functools.partial(source_kernel, far, peers),
        out_shape=jax.ShapeDtypeStruct((peers, per_peer, time), BF16 if far else F32),
        in_specs=[smem] + [vmem] * (2 + len(ins) + len(extra)),
        out_specs=vmem,
        scratch_shapes=[pltpu.VMEM((peers // 2, time // LANES, per_peer, LANES), F32)],
        name="source_far" if far else "source_near",
    )(taper, delay, frac, *ins, *extra)


def body(traces, rcv_delay, rcv_frac, live_count, src_delay, src_frac, rcv_taper, src_taper):
    rows, time = traces.shape[1:]
    peers = lax.axis_size("shot")
    groups = lax.axis_size("rcv")
    here = lax.axis_index("rcv")
    per_peer = rows // peers
    traces = traces[0]
    edge_rows = 16
    edge = lax.ppermute(
        lax.dynamic_slice_in_dim(traces, (1 - here) * (rows - edge_rows), edge_rows, 0),
        "rcv",
        [(0, 1), (1, 0)],
    )

    args = (live_count, rcv_taper, traces, edge, rcv_delay[0], rcv_frac[0])
    far_out = receiver_side(True, peers, *args)
    far_in = [swap(far_out[r], r + peers // 2, peers) for r in range(peers // 2)]
    near_out = receiver_side(False, peers, *args)
    near_in = [near_out[0]] + [swap(near_out[r], r, peers) for r in range(1, peers // 2)]
    delay, frac = src_delay[:, 0], src_frac[:, 0]
    partial = source_side(False, peers, src_taper, delay, frac, near_in)
    result = source_side(True, peers, src_taper, delay, frac, far_in, partial)
    return result.reshape(peers, 1, per_peer, time)


def swap(block, step, peers):
    return lax.ppermute(block, "shot", [(i, i ^ step) for i in range(peers)])


def solution(mesh):
    return jax.shard_map(
        body,
        mesh=mesh,
        in_specs=(
            P(("slab", "shot"), "rcv", None),
            P(("slab", "shot"), "rcv", None),
            P(("slab", "shot"), "rcv", None),
            P(("slab", "shot")),
            P("slab", "rcv", "shot", None),
            P("slab", "rcv", "shot", None),
            P(),
            P(),
        ),
        out_specs=P("slab", "rcv", "shot", None),
        check_vma=False,
    )
```

```python
import functools
import math

import jax
import jax.numpy as jnp
from jax import lax
from jax.experimental import pallas as pl
from jax.experimental.pallas import tpu as pltpu
from jax.sharding import PartitionSpec as P

AR = 4
AS = 4
TRI = 2
KR = 9
KS = 9
LANES = 128
F32 = jnp.float32
BF16 = jnp.bfloat16


def filter_band():
    rows = lax.broadcasted_iota(jnp.int32, (3 * LANES, LANES), 0) - LANES
    cols = lax.broadcasted_iota(jnp.int32, (3 * LANES, LANES), 1)
    height = jnp.maximum(TRI - jnp.abs(cols - rows), 0).astype(F32)
    energy = float(sum((TRI - abs(m)) ** 2 for m in range(1 - TRI, TRI)))
    return (height / math.sqrt(energy)).astype(BF16)


def filtered_block(source, block, blocks, band):
    low, high = max(block - 1, 0), min(block + 2, blocks)
    part = source[:, low * LANES : high * LANES]
    start = (low - block + 1) * LANES
    dot = jnp.dot(part, band[start : start + (high - low) * LANES], preferred_element_type=F32)
    return dot.astype(BF16).astype(F32)


def spread(table, taps):
    row = lax.broadcasted_iota(jnp.int32, (taps, taps * LANES), 0)
    col = lax.broadcasted_iota(jnp.int32, (taps, taps * LANES), 1)
    pick = (col // LANES == row).astype(BF16)
    dims = (((0,), (0,)), ((), ()))
    return lax.dot_general(table.astype(F32).astype(BF16), pick, dims, preferred_element_type=F32)


def add_tap(first, second, load, blocks, delay, frac, taper, lane):
    place = lane + delay.astype(jnp.int32)
    index = place & (LANES - 1)
    here = place < LANES
    two = frac * (taper * (1.0 / 256.0))
    one = taper - two
    moved = [jnp.take_along_axis(load(b), index, axis=1, mode="promise_in_bounds") for b in range(blocks)]
    moved.append(jnp.zeros_like(moved[0]))
    for b in range(blocks):
        value = jnp.where(here, moved[b], moved[b + 1])
        first[b] = first[b] + one * value
        second[b] = second[b] + two * value


def join(first, second, blocks, lane):
    rolled = [pltpu.roll(v, LANES - 1, 1) for v in second] + [jnp.zeros_like(second[0])]
    inner = lane < LANES - 1
    return [first[b] + jnp.where(inner, rolled[b], rolled[b + 1]) for b in range(blocks)]


def receiver_kernel(far, peers, live_ref, taper_ref, traces_ref, edge_ref, delay_ref, frac_ref, out_ref, src_ref, wide_ref):
    rows, time = traces_ref.shape
    blocks = time // LANES
    halves = 2
    part = rows // halves
    per_peer = rows // peers
    group = min(8, per_peer)
    me = lax.axis_index("shot")
    mine = me // (peers // 2)
    half = (1 - mine) if far else mine
    low = me % (peers // 2)
    block_of = lax.axis_index("rcv")
    groups = lax.axis_size("rcv")
    base = pl.multiple_of(half * part, part)
    edge = edge_ref.shape[0]

    left_in = traces_ref[pl.ds(pl.multiple_of(jnp.maximum(base - edge, 0), edge), edge), :]
    right_in = traces_ref[pl.ds(pl.multiple_of(jnp.minimum(base + part, rows - edge), edge), edge), :]
    other = edge_ref[...]
    left = jnp.where(half == 0, other, left_in)
    right = jnp.where(half == halves - 1, other, right_in)
    source = jnp.concatenate([left, traces_ref[pl.ds(base, part), :], right], axis=0)
    height = part + 2 * edge
    where = lax.broadcasted_iota(jnp.int32, (height, LANES), 0) + (block_of * rows + base - edge)
    live = live_ref[0]
    alive = (where >= 0) & (where < rows * groups) & (where < live)
    band = filter_band()
    for b in range(blocks):
        src_ref[b] = jnp.where(alive, filtered_block(source, b, blocks, band), 0.0)

    for i, table in enumerate((delay_ref, frac_ref)):
        wide = spread(table[...], KR)
        for a in range(KR):
            wide_ref[i, a] = wide[:, a * LANES : (a + 1) * LANES]
    lane = lax.broadcasted_iota(jnp.int32, (8, LANES), 1)
    line = lax.broadcasted_iota(jnp.int32, (8, LANES), 0)
    last = jnp.minimum(live, rows * groups) - 1
    for g in range(part // 8):
        at = pl.ds(pl.multiple_of(base + g * 8, 8), 8)
        first = [jnp.zeros((8, LANES), F32) for _ in range(blocks)]
        second = [jnp.zeros((8, LANES), F32) for _ in range(blocks)]
        for a in range(KR):
            row = edge + g * 8 + a - AR
            add_tap(
                first,
                second,
                lambda b: src_ref[b, row : row + 8, :],
                blocks,
                wide_ref[0, a, at, :],
                wide_ref[1, a, at, :],
                taper_ref[a],
                lane,
            )
        here = line + (block_of * rows + base + g * 8)
        fold = jnp.minimum(here + AR, last) - jnp.maximum(here - AR, 0) + 1
        scale = 1.0 / jnp.sqrt(jnp.maximum(fold, 1).astype(F32))
        total = join(first, second, blocks, lane)
        for s in range(8 // group):
            row = g * 8 + s * group
            peer = (row // per_peer) ^ low
            for b in range(blocks):
                value = (total[b] * scale).astype(BF16)[s * group : (s + 1) * group]
                out_ref[peer, row % per_peer : row % per_peer + group, b * LANES : (b + 1) * LANES] = value


def receiver_side(far, peers, live, taper, traces, edge, delay, frac):
    rows, time = traces.shape
    vmem = pl.BlockSpec(memory_space=pltpu.VMEM)
    smem = pl.BlockSpec(memory_space=pltpu.SMEM)
    return pl.pallas_call(
        functools.partial(receiver_kernel, far, peers),
        out_shape=jax.ShapeDtypeStruct((peers // 2, rows // peers, time), BF16),
        in_specs=[smem, smem, vmem, vmem, vmem, vmem],
        out_specs=vmem,
        scratch_shapes=[
            pltpu.VMEM((time // LANES, rows // 2 + 2 * edge.shape[0], LANES), F32),
            pltpu.VMEM((2, KR, rows, LANES), F32),
        ],
        compiler_params=pltpu.CompilerParams(vmem_limit_bytes=24 << 20),
        name="receiver_far" if far else "receiver_near",
    )(live, taper, traces, edge, delay, frac)


def source_kernel(far, peers, taper_ref, delay_ref, frac_ref, *refs):
    half_peers = peers // 2
    ins = refs[:half_peers]
    refs = refs[half_peers:]
    if far:
        part_ref, out_ref, src_ref, wide_ref = refs
    else:
        out_ref, src_ref, wide_ref = refs
    per_peer, time = ins[0].shape
    blocks = time // LANES
    me = lax.axis_index("shot")
    mine = me // half_peers
    half = (1 - mine) if far else mine
    low = me % half_peers
    flip = half == 1
    band = filter_band()
    for r in range(half_peers):
        near = low ^ r
        slot = jnp.where(flip, half_peers - 1 - near, near)
        source = ins[r][...]
        for b in range(blocks):
            src_ref[slot, b] = filtered_block(source, b, blocks, band)
    for i, table in enumerate((delay_ref, frac_ref)):
        for k in range(peers):
            wide = spread(table[k], KS)
            for a in range(KS):
                wide_ref[i, k, a] = wide[:, a * LANES : (a + 1) * LANES]
    rows = min(8, per_peer)
    lane = lax.broadcasted_iota(jnp.int32, (rows, LANES), 1)
    for kk in range(peers):
        k = jnp.where(flip, peers - 1 - kk, kk)
        near = [pp for pp in range(half_peers) if abs(pp - kk) <= AS]
        count = min(kk + AS, peers - 1) - max(kk - AS, 0) + 1
        for i in range(per_peer // rows):
            at = slice(i * rows, (i + 1) * rows)
            first = [jnp.zeros((rows, LANES), F32) for _ in range(blocks)]
            second = [jnp.zeros((rows, LANES), F32) for _ in range(blocks)]
            for pp in near:
                up, down = pp - kk + AS, kk - pp + AS
                tap = jnp.where(flip, down, up)
                add_tap(
                    first,
                    second,
                    lambda b: src_ref[pp, b, at, :],
                    blocks,
                    wide_ref[0, k, tap, at, :],
                    wide_ref[1, k, tap, at, :],
                    taper_ref[tap],
                    lane,
                )
            total = join(first, second, blocks, lane) if near else first
            for b in range(blocks):
                cols = slice(b * LANES, (b + 1) * LANES)
                value = total[b]
                if far:
                    value = (value + part_ref[k, at, cols]) * (1.0 / math.sqrt(count))
                out_ref[k, at, cols] = value.astype(out_ref.dtype)


def source_side(far, peers, taper, delay, frac, ins, partial=None):
    per_peer, time = ins[0].shape
    vmem = pl.BlockSpec(memory_space=pltpu.VMEM)
    smem = pl.BlockSpec(memory_space=pltpu.SMEM)
    extra = [partial] if far else []
    return pl.pallas_call(
        functools.partial(source_kernel, far, peers),
        out_shape=jax.ShapeDtypeStruct((peers, per_peer, time), BF16 if far else F32),
        in_specs=[smem] + [vmem] * (2 + len(ins) + len(extra)),
        out_specs=vmem,
        scratch_shapes=[
            pltpu.VMEM((peers // 2, time // LANES, per_peer, LANES), F32),
            pltpu.VMEM((2, peers, KS, per_peer, LANES), F32),
        ],
        compiler_params=pltpu.CompilerParams(vmem_limit_bytes=24 << 20),
        name="source_far" if far else "source_near",
    )(taper, delay, frac, *ins, *extra)


def body(traces, rcv_delay, rcv_frac, live_count, src_delay, src_frac, rcv_taper, src_taper):
    rows, time = traces.shape[1:]
    peers = lax.axis_size("shot")
    groups = lax.axis_size("rcv")
    here = lax.axis_index("rcv")
    per_peer = rows // peers
    traces = traces[0]
    edge_rows = 16
    edge = lax.ppermute(
        lax.dynamic_slice_in_dim(traces, (1 - here) * (rows - edge_rows), edge_rows, 0),
        "rcv",
        [(0, 1), (1, 0)],
    )

    args = (live_count, rcv_taper, traces, edge, rcv_delay[0].T, rcv_frac[0].T)
    far_out = receiver_side(True, peers, *args)
    far_in = [swap(far_out[r], r + peers // 2, peers) for r in range(peers // 2)]
    near_out = receiver_side(False, peers, *args)
    near_in = [near_out[0]] + [swap(near_out[r], r, peers) for r in range(1, peers // 2)]
    delay, frac = (jnp.transpose(v[:, 0], (0, 2, 1)) for v in (src_delay, src_frac))
    partial = source_side(False, peers, src_taper, delay, frac, near_in)
    result = source_side(True, peers, src_taper, delay, frac, far_in, partial)
    return result.reshape(peers, 1, per_peer, time)


def swap(block, step, peers):
    return lax.ppermute(block, "shot", [(i, i ^ step) for i in range(peers)])


def solution(mesh):
    return jax.shard_map(
        body,
        mesh=mesh,
        in_specs=(
            P(("slab", "shot"), "rcv", None),
            P(("slab", "shot"), "rcv", None),
            P(("slab", "shot"), "rcv", None),
            P(("slab", "shot")),
            P("slab", "rcv", "shot", None),
            P("slab", "rcv", "shot", None),
            P(),
            P(),
        ),
        out_specs=P("slab", "rcv", "shot", None),
        check_vma=False,
    )
```

```python
import functools
import math

import jax
import jax.numpy as jnp
from jax import lax
from jax.experimental import pallas as pl
from jax.experimental.pallas import tpu as pltpu
from jax.sharding import PartitionSpec as P

AR = 4
AS = 4
TRI = 2
KR = 9
KS = 9
LANES = 128
SUB = 8
EDGE = 16
F32 = jnp.float32
BF16 = jnp.bfloat16
I32 = jnp.int32
GRANT = 24 << 20


def iota(shape, axis):
    return lax.broadcasted_iota(I32, shape, axis)


def filter_band():
    away = jnp.abs(iota((3 * LANES, LANES), 1) - (iota((3 * LANES, LANES), 0) - LANES))
    energy = float(sum((TRI - abs(m)) ** 2 for m in range(1 - TRI, TRI)))
    return (jnp.maximum(TRI - away, 0).astype(F32) / math.sqrt(energy)).astype(BF16)


def filtered_block(source, block, blocks, band):
    low, high = max(block - 1, 0), min(block + 2, blocks)
    part = source[:, low * LANES : high * LANES]
    start = (low - block + 1) * LANES
    dot = jnp.dot(part, band[start : start + (high - low) * LANES], preferred_element_type=F32)
    return dot.astype(BF16).astype(F32)


def spread(table, pick):
    dims = (((0,), (0,)), ((), ()))
    return lax.dot_general(table.astype(F32).astype(BF16), pick.astype(BF16), dims, preferred_element_type=F32)


def weight_parts(frac, taper, keep):
    two = jnp.where(keep, frac * (taper * (1.0 / 256.0)), 0.0)
    one = jnp.where(keep, taper, 0.0) - two
    parts = []
    for value in (one, two):
        high = value.astype(BF16).astype(F32)
        parts += [high, value - high]
    return parts


def shifted(load, place, blocks):
    index = place & (LANES - 1)
    here = place < LANES
    moved = [jnp.take_along_axis(load(b), index, axis=1, mode="promise_in_bounds") for b in range(blocks)]
    moved.append(jnp.zeros_like(moved[0]))
    return [jnp.where(here, moved[b], moved[b + 1]) for b in range(blocks)]


def weighted(weights, taps, blocks, rows, lane):
    first, second = [], []
    for b in range(blocks):
        stack = jnp.concatenate([tap[b] for tap in taps], axis=0).astype(BF16)
        dot = jnp.dot(weights, stack, preferred_element_type=F32)
        first.append(dot[:rows] + dot[rows : 2 * rows])
        second.append(dot[2 * rows : 3 * rows] + dot[3 * rows :])
    rolled = [pltpu.roll(v, LANES - 1, 1) for v in second] + [jnp.zeros_like(second[0])]
    inner = lane < LANES - 1
    return [first[b] + jnp.where(inner, rolled[b], rolled[b + 1]) for b in range(blocks)]


def receiver_tables_kernel(live_ref, taper_ref, delay_ref, frac_ref, place_ref, weight_ref):
    rows = delay_ref.shape[1]
    for a in range(KR):
        pick = iota((KR, LANES), 0) == a
        place_ref[a] = iota((rows, LANES), 1) + spread(delay_ref[...], pick).astype(I32)
    wide = (rows, LANES)
    tap = iota((KR, LANES), 1) // SUB == iota((KR, LANES), 0)
    frac = spread(frac_ref[...], tap)
    row, lane = iota(wide, 0), iota(wide, 1)
    line = row + lax.axis_index("rcv") * rows
    live = jnp.minimum(live_ref[0], rows * lax.axis_size("rcv"))
    source = line + lane // SUB - AR
    keep = (lane % SUB == row % SUB) & (lane < KR * SUB) & (source >= 0) & (source < live)
    fold = jnp.minimum(line + AR, live - 1) - jnp.maximum(line - AR, 0) + 1
    taper = jnp.zeros(wide, F32)
    for a in range(KR):
        taper = jnp.where(lane // SUB == a, taper_ref[a], taper)
    taper = taper / jnp.sqrt(jnp.maximum(fold, 1).astype(F32))
    for i, part in enumerate(weight_parts(frac, taper, keep)):
        weight_ref[i] = part


def receiver_kernel(far, peers, traces_ref, edge_ref, place_ref, weight_ref, out_ref, src_ref):
    rows, time = traces_ref.shape
    blocks = time // LANES
    part = rows // 2
    per_peer = rows // peers
    me = lax.axis_index("shot")
    mine = me // (peers // 2)
    half = (1 - mine) if far else mine
    low = me % (peers // 2)
    base = pl.multiple_of(half * part, part)

    left_in = traces_ref[pl.ds(pl.multiple_of(jnp.maximum(base - EDGE, 0), EDGE), EDGE), :]
    right_in = traces_ref[pl.ds(pl.multiple_of(jnp.minimum(base + part, rows - EDGE), EDGE), EDGE), :]
    other = edge_ref[...]
    left = jnp.where(half == 0, other, left_in)
    right = jnp.where(half == 1, other, right_in)
    source = jnp.concatenate([left, traces_ref[pl.ds(base, part), :], right], axis=0)
    band = filter_band()
    for b in range(blocks):
        src_ref[b] = filtered_block(source, b, blocks, band)

    lane = iota((SUB, LANES), 1)
    totals = []
    for g in range(part // SUB):
        at = pl.ds(pl.multiple_of(base + g * SUB, SUB), SUB)
        taps = []
        for a in range(KR):
            row = EDGE + g * SUB + a - AR
            taps.append(shifted(lambda b: src_ref[b, row : row + SUB, :], place_ref[a, at, :], blocks))
        weights = jnp.concatenate([weight_ref[i, at, : KR * SUB] for i in range(4)], axis=0).astype(BF16)
        totals.append(weighted(weights, taps, blocks, SUB, lane))
        step = max(1, min(2, per_peer // SUB))
        if len(totals) < step:
            continue
        first = (g + 1 - step) * SUB
        for s in range(0, step * SUB, min(step * SUB, per_peer)):
            height = min(step * SUB, per_peer)
            peer = ((first + s) // per_peer) ^ low
            start = (first + s) % per_peer
            for b in range(blocks):
                value = jnp.concatenate([t[b] for t in totals], axis=0).astype(BF16)
                out_ref[peer, start : start + height, b * LANES : (b + 1) * LANES] = value[s : s + height]
        totals = []


def source_tables_kernel(peers, taper_ref, delay_ref, frac_ref, place_ref, weight_ref):
    half_peers = peers // 2
    rows = delay_ref.shape[2]
    wide = half_peers * rows
    mine = lax.axis_index("shot") // half_peers
    for far in range(2):
        flip = mine == 1 - far
        sign = jnp.where(flip, -1, 1)
        for kk in range(peers):
            k = jnp.where(flip, peers - 1 - kk, kk)
            delay, frac = delay_ref[k], frac_ref[k]
            count = min(kk + AS, peers - 1) - max(kk - AS, 0) + 1
            row, lane = iota((rows, wide), 0), iota((rows, wide), 1)
            taper = jnp.zeros((rows, wide), F32)
            for pp in range(half_peers):
                if abs(pp - kk) <= AS:
                    tap = AS + sign * (pp - kk)
                    pick = iota((KS, LANES), 0) == tap
                    place_ref[far, kk, pp] = iota((rows, LANES), 1) + spread(delay, pick).astype(I32)
                    taper = jnp.where(lane // rows == pp, taper_ref[tap], taper)
            tap = AS + sign * (iota((KS, wide), 1) // rows - kk)
            keep = lane % rows == row
            parts = weight_parts(spread(frac, iota((KS, wide), 0) == tap), taper * (1.0 / math.sqrt(count)), keep)
            weight_ref[far, kk] = jnp.concatenate(parts, axis=0).astype(BF16)


def source_kernel(far, peers, place_ref, weight_ref, *refs):
    half_peers = peers // 2
    ins = refs[:half_peers]
    refs = refs[half_peers:]
    if far:
        part_ref, out_ref, src_ref = refs
    else:
        out_ref, src_ref = refs
    per_peer, time = ins[0].shape
    blocks = time // LANES
    me = lax.axis_index("shot")
    mine = me // half_peers
    half = (1 - mine) if far else mine
    low = me % half_peers
    flip = half == 1
    band = filter_band()
    for r in range(half_peers):
        near = low ^ r
        slot = jnp.where(flip, half_peers - 1 - near, near)
        source = ins[r][...]
        for b in range(blocks):
            src_ref[slot, b] = filtered_block(source, b, blocks, band)
    rows = min(SUB, per_peer)
    lane = iota((per_peer, LANES), 1)
    for kk in range(peers):
        k = jnp.where(flip, peers - 1 - kk, kk)
        near = [pp for pp in range(half_peers) if abs(pp - kk) <= AS]
        if near:
            taps = []
            for pp in near:
                for i in range(0, per_peer, rows):
                    at = slice(i, i + rows)
                    taps.append(shifted(lambda b: src_ref[pp, b, at, :], place_ref[far, kk, pp, at, :], blocks))
            weights = weight_ref[far, kk, :, near[0] * per_peer : (near[-1] + 1) * per_peer]
            total = weighted(weights, taps, blocks, per_peer, lane)
        else:
            total = [jnp.zeros((per_peer, LANES), F32)] * blocks
        for b in range(blocks):
            cols = slice(b * LANES, (b + 1) * LANES)
            value = total[b]
            if far:
                value = value + part_ref[k, :, cols]
            out_ref[k, :, cols] = value.astype(out_ref.dtype)


VMEM = pl.BlockSpec(memory_space=pltpu.VMEM)
SMEM = pl.BlockSpec(memory_space=pltpu.SMEM)


def call(kernel, name, args, specs, outs, scratch=(), cost=0):
    return pl.pallas_call(
        kernel,
        out_shape=outs,
        in_specs=specs,
        out_specs=[VMEM] * len(outs) if isinstance(outs, tuple) else VMEM,
        scratch_shapes=list(scratch),
        compiler_params=pltpu.CompilerParams(vmem_limit_bytes=GRANT),
        name=name,
    )(*args)


def body(traces, rcv_delay, rcv_frac, live_count, src_delay, src_frac, rcv_taper, src_taper):
    rows, time = traces.shape[1:]
    blocks = time // LANES
    peers = lax.axis_size("shot")
    half_peers = peers // 2
    here = lax.axis_index("rcv")
    per_peer = rows // peers
    traces = traces[0]
    edge = lax.ppermute(
        lax.dynamic_slice_in_dim(traces, (1 - here) * (rows - EDGE), EDGE, 0), "rcv", [(0, 1), (1, 0)]
    )
    shape = jax.ShapeDtypeStruct

    tables = call(
        receiver_tables_kernel,
        "receiver_tables",
        (live_count, rcv_taper, rcv_delay[0].T, rcv_frac[0].T),
        [SMEM, SMEM, VMEM, VMEM],
        (shape((KR, rows, LANES), I32), shape((4, rows, LANES), F32)),
    )
    source_tables = call(
        functools.partial(source_tables_kernel, peers),
        "source_tables",
        (src_taper, *(jnp.transpose(v[:, 0], (0, 2, 1)) for v in (src_delay, src_frac))),
        [SMEM, VMEM, VMEM],
        (
            shape((2, peers, half_peers, per_peer, LANES), I32),
            shape((2, peers, 4 * per_peer, half_peers * per_peer), BF16),
        ),
    )

    def receivers(far):
        return call(
            functools.partial(receiver_kernel, far, peers),
            "receiver_far" if far else "receiver_near",
            (traces, edge, *tables),
            [VMEM] * 4,
            shape((half_peers, per_peer, time), BF16),
            [pltpu.VMEM((blocks, rows // 2 + 2 * EDGE, LANES), F32)],
        )

    def sources(far, ins, partial=()):
        return call(
            functools.partial(source_kernel, far, peers),
            "source_far" if far else "source_near",
            (*source_tables, *ins, *partial),
            [VMEM] * (2 + len(ins) + len(partial)),
            shape((peers, per_peer, time), BF16 if far else F32),
            [pltpu.VMEM((half_peers, blocks, per_peer, LANES), F32)],
        )

    far_out = receivers(1)
    far_in = [swap(far_out[r], r + half_peers, peers) for r in range(half_peers)]
    near_out = receivers(0)
    near_in = [near_out[0]] + [swap(near_out[r], r, peers) for r in range(1, half_peers)]
    partial = sources(0, near_in)
    result = sources(1, far_in, (partial,))
    return result.reshape(peers, 1, per_peer, time)


def swap(block, step, peers):
    return lax.ppermute(block, "shot", [(i, i ^ step) for i in range(peers)])


def solution(mesh):
    return jax.shard_map(
        body,
        mesh=mesh,
        in_specs=(
            P(("slab", "shot"), "rcv", None),
            P(("slab", "shot"), "rcv", None),
            P(("slab", "shot"), "rcv", None),
            P(("slab", "shot")),
            P("slab", "rcv", "shot", None),
            P("slab", "rcv", "shot", None),
            P(),
            P(),
        ),
        out_specs=P("slab", "rcv", "shot", None),
        check_vma=False,
    )
```

```python
import functools
import math

import jax
import jax.numpy as jnp
from jax import lax
from jax.experimental import pallas as pl
from jax.experimental.pallas import tpu as pltpu
from jax.sharding import PartitionSpec as P


AR = 4
AS = 4
TRI = 2
KR = 9
KS = 9
LANES = 128
SUB = 8
EDGE = 16
F32 = jnp.float32
BF16 = jnp.bfloat16
I32 = jnp.int32
GRANT = 24 << 20


def iota(shape, axis):
    return lax.broadcasted_iota(I32, shape, axis)


def filter_band(width):
    height = width + 2 * LANES
    away = jnp.abs(iota((height, width), 1) - (iota((height, width), 0) - LANES))
    energy = float(sum((TRI - abs(m)) ** 2 for m in range(1 - TRI, TRI)))
    return (jnp.maximum(TRI - away, 0).astype(F32) / math.sqrt(energy)).astype(BF16)


def pair_of(blocks):
    return 2 if blocks % 2 == 0 else 1


def filtered(source, band, store):
    blocks = source.shape[1] // LANES
    step = pair_of(blocks)
    for b in range(0, blocks, step):
        low, high = max(b - 1, 0), min(b + step + 1, blocks)
        start = (low - b + 1) * LANES
        part = source[:, low * LANES : high * LANES]
        dot = jnp.dot(part, band[start : start + (high - low) * LANES, :], preferred_element_type=F32)
        value = dot.astype(BF16).astype(F32)
        for i in range(step):
            store(b + i, value[:, i * LANES : (i + 1) * LANES])


def filtered_few(source, band):
    rows, time = source.shape
    blank = jnp.zeros((rows, LANES), BF16)
    wide = jnp.concatenate([blank, source, blank], axis=1)
    stack = jnp.concatenate([wide[:, t : t + 3 * LANES] for t in range(0, time, LANES)], axis=0)
    dot = jnp.dot(stack, band[: 3 * LANES, :LANES], preferred_element_type=F32).astype(BF16).astype(F32)
    return [dot[i : i + rows] for i in range(0, dot.shape[0], rows)]


def spread(table, pick):
    dims = (((0,), (0,)), ((), ()))
    return lax.dot_general(table.astype(F32).astype(BF16), pick.astype(BF16), dims, preferred_element_type=F32)


def weight_parts(frac, taper, keep):
    two = jnp.where(keep, frac * (taper * (1.0 / 256.0)), 0.0)
    one = jnp.where(keep, taper, 0.0) - two
    parts = []
    for value in (one, two):
        high = value.astype(BF16).astype(F32)
        parts += [high, value - high]
    return parts


def shifted(load, place, blocks):
    index = place & (LANES - 1)
    here = place < LANES
    moved = [jnp.take_along_axis(load(b), index, axis=1, mode="promise_in_bounds") for b in range(blocks)]
    moved.append(jnp.zeros_like(moved[0]))
    return [jnp.where(here, moved[b], moved[b + 1]) for b in range(blocks)]


def weighted(weights, taps, blocks, rows, lane):
    first, second = [], []
    step = pair_of(blocks)
    for b in range(0, blocks, step):
        stack = jnp.concatenate(
            [jnp.concatenate([tap[b + i] for tap in taps], axis=0).astype(BF16) for i in range(step)], axis=1
        )
        dot = jnp.dot(weights, stack, preferred_element_type=F32)
        for i in range(step):
            cols = slice(i * LANES, (i + 1) * LANES)
            first.append(dot[:rows, cols] + dot[rows : 2 * rows, cols])
            second.append(dot[2 * rows : 3 * rows, cols] + dot[3 * rows :, cols])
    rolled = [pltpu.roll(v, LANES - 1, 1) for v in second] + [jnp.zeros_like(second[0])]
    inner = lane < LANES - 1
    return [first[b] + jnp.where(inner, rolled[b], rolled[b + 1]) for b in range(blocks)]


def receiver_tables_kernel(
    live_in, taper_in, traces_in, delay_ref, frac_ref, place_ref, weight_ref, filt_ref, band_ref, live_ref, taper_ref, traces_ref, sem
):
    copies = [
        pltpu.make_async_copy(source, target, sem.at[i])
        for i, (source, target) in enumerate(((traces_in, traces_ref), (live_in, live_ref), (taper_in, taper_ref)))
    ]
    for copy in copies:
        copy.start()
    rows = delay_ref.shape[1]
    band_ref[...] = filter_band(band_ref.shape[1])
    for a in range(KR):
        pick = iota((KR, LANES), 0) == a
        place_ref[a] = iota((rows, LANES), 1) + spread(delay_ref[...], pick).astype(I32)
    wide = (rows, LANES)
    tap = iota((KR, LANES), 1) // SUB == iota((KR, LANES), 0)
    frac = spread(frac_ref[...], tap)
    row, lane = iota(wide, 0), iota(wide, 1)
    line = row + lax.axis_index("rcv") * rows
    copies[1].wait()
    copies[2].wait()
    live = jnp.minimum(live_ref[0], rows * lax.axis_size("rcv"))
    source = line + lane // SUB - AR
    keep = (lane % SUB == row % SUB) & (lane < KR * SUB) & (source >= 0) & (source < live)
    fold = jnp.minimum(line + AR, live - 1) - jnp.maximum(line - AR, 0) + 1
    taper = jnp.zeros(wide, F32)
    for a in range(KR):
        taper = jnp.where(lane // SUB == a, taper_ref[a], taper)
    taper = taper / jnp.sqrt(jnp.maximum(fold, 1).astype(F32))
    for i, part in enumerate(weight_parts(frac, taper, keep)):
        weight_ref[i] = part

    def store(b, value):
        filt_ref[b] = value

    copies[0].wait()
    filtered(traces_ref[...], band_ref, store)


def receiver_kernel(far, peers, other_ref, place_ref, weight_ref, filt_ref, band_ref, out_ref, src_ref):
    blocks, rows = filt_ref.shape[:2]
    part = rows // 2
    per_peer = rows // peers
    me = lax.axis_index("shot")
    mine = me // (peers // 2)
    half = (1 - mine) if far else mine
    low = me % (peers // 2)
    base = pl.multiple_of(half * part, part)

    left_at = pl.ds(pl.multiple_of(jnp.maximum(base - EDGE, 0), EDGE), EDGE)
    right_at = pl.ds(pl.multiple_of(jnp.minimum(base + part, rows - EDGE), EDGE), EDGE)
    far_side = pl.multiple_of(jnp.where(half == 0, rows - EDGE, 0), EDGE)
    other = filtered_few(other_ref[pl.ds(far_side, EDGE), :], band_ref)
    for b in range(blocks):
        src_ref[b, :EDGE] = jnp.where(half == 0, other[b], filt_ref[b, left_at, :])
        src_ref[b, EDGE : EDGE + part] = filt_ref[b, pl.ds(base, part), :]
        src_ref[b, EDGE + part :] = jnp.where(half == 1, other[b], filt_ref[b, right_at, :])

    lane = iota((SUB, LANES), 1)
    totals = []
    for g in range(part // SUB):
        at = pl.ds(pl.multiple_of(base + g * SUB, SUB), SUB)
        taps = []
        for a in range(KR):
            row = EDGE + g * SUB + a - AR
            taps.append(shifted(lambda b: src_ref[b, row : row + SUB, :], place_ref[a, at, :], blocks))
        weights = jnp.concatenate([weight_ref[i, at, : KR * SUB] for i in range(4)], axis=0).astype(BF16)
        totals.append(weighted(weights, taps, blocks, SUB, lane))
        step = max(1, min(2, per_peer // SUB))
        if len(totals) < step:
            continue
        first = (g + 1 - step) * SUB
        for s in range(0, step * SUB, min(step * SUB, per_peer)):
            height = min(step * SUB, per_peer)
            peer = ((first + s) // per_peer) ^ low
            start = (first + s) % per_peer
            for b in range(blocks):
                value = jnp.concatenate([t[b] for t in totals], axis=0).astype(BF16)
                out_ref[peer, start : start + height, b * LANES : (b + 1) * LANES] = value[s : s + height]
        totals = []


def source_tables_kernel(peers, taper_in, delay_ref, frac_ref, place_ref, weight_ref, taper_ref, sem):
    copy = pltpu.make_async_copy(taper_in, taper_ref, sem)
    copy.start()
    copy.wait()
    half_peers = peers // 2
    rows = delay_ref.shape[2]
    wide = half_peers * rows
    mine = lax.axis_index("shot") // half_peers
    for far in range(2):
        flip = mine == 1 - far
        sign = jnp.where(flip, -1, 1)
        for kk in range(peers):
            k = jnp.where(flip, peers - 1 - kk, kk)
            delay, frac = delay_ref[k], frac_ref[k]
            count = min(kk + AS, peers - 1) - max(kk - AS, 0) + 1
            row, lane = iota((rows, wide), 0), iota((rows, wide), 1)
            taper = jnp.zeros((rows, wide), F32)
            for pp in range(half_peers):
                if abs(pp - kk) <= AS:
                    tap = AS + sign * (pp - kk)
                    pick = iota((KS, LANES), 0) == tap
                    place_ref[far, kk, pp] = iota((rows, LANES), 1) + spread(delay, pick).astype(I32)
                    taper = jnp.where(lane // rows == pp, taper_ref[tap], taper)
            tap = AS + sign * (iota((KS, wide), 1) // rows - kk)
            keep = lane % rows == row
            parts = weight_parts(spread(frac, iota((KS, wide), 0) == tap), taper * (1.0 / math.sqrt(count)), keep)
            weight_ref[far, kk] = jnp.concatenate(parts, axis=0).astype(BF16)


def source_kernel(far, peers, place_ref, weight_ref, band_ref, *refs):
    half_peers = peers // 2
    ins = refs[:half_peers]
    refs = refs[half_peers:]
    if far:
        part_ref, out_ref, src_ref = refs
    else:
        out_ref, src_ref = refs
    per_peer, time = ins[0].shape
    blocks = time // LANES
    me = lax.axis_index("shot")
    mine = me // half_peers
    half = (1 - mine) if far else mine
    low = me % half_peers
    flip = half == 1
    slots = [jnp.where(flip, half_peers - 1 - (low ^ r), low ^ r) for r in range(half_peers)]

    def store(b, value):
        for r in range(half_peers):
            src_ref[slots[r], b] = value[r * per_peer : (r + 1) * per_peer]

    filtered(jnp.concatenate([ref[...] for ref in ins], axis=0), band_ref, store)
    rows = min(SUB, per_peer)
    lane = iota((per_peer, LANES), 1)
    for kk in range(peers):
        k = jnp.where(flip, peers - 1 - kk, kk)
        near = [pp for pp in range(half_peers) if abs(pp - kk) <= AS]
        if near:
            taps = []
            for pp in near:
                for i in range(0, per_peer, rows):
                    at = slice(i, i + rows)
                    taps.append(shifted(lambda b: src_ref[pp, b, at, :], place_ref[far, kk, pp, at, :], blocks))
            weights = weight_ref[far, kk, :, near[0] * per_peer : (near[-1] + 1) * per_peer]
            total = weighted(weights, taps, blocks, per_peer, lane)
        else:
            total = [jnp.zeros((per_peer, LANES), F32)] * blocks
        for b in range(blocks):
            cols = slice(b * LANES, (b + 1) * LANES)
            value = total[b]
            if far:
                value = value + part_ref[k, :, cols]
            out_ref[k, :, cols] = value.astype(out_ref.dtype)


VMEM = pl.BlockSpec(memory_space=pltpu.VMEM)
HBM = pl.BlockSpec(memory_space=pltpu.HBM)


def call(kernel, args, specs, outs, scratch=()):
    return pl.pallas_call(
        kernel,
        out_shape=outs,
        in_specs=specs,
        out_specs=[VMEM] * len(outs) if isinstance(outs, tuple) else VMEM,
        scratch_shapes=list(scratch),
        compiler_params=pltpu.CompilerParams(vmem_limit_bytes=GRANT),
    )(*args)


def body(traces, rcv_delay, rcv_frac, live_count, src_delay, src_frac, rcv_taper, src_taper):
    rows, time = traces.shape[1:]
    blocks = time // LANES
    peers = lax.axis_size("shot")
    half_peers = peers // 2
    per_peer = rows // peers
    traces = traces[0]
    other = lax.ppermute(traces, "rcv", [(0, 1), (1, 0)])
    shape = jax.ShapeDtypeStruct
    width = pair_of(blocks) * LANES

    place, weight, filt, band = call(
        receiver_tables_kernel,
        (live_count, rcv_taper, traces, rcv_delay[0].T, rcv_frac[0].T),
        [HBM, HBM, HBM, VMEM, VMEM],
        (
            shape((KR, rows, LANES), I32),
            shape((4, rows, LANES), F32),
            shape((blocks, rows, LANES), F32),
            shape((width + 2 * LANES, width), BF16),
        ),
        [
            pltpu.SMEM(live_count.shape, I32),
            pltpu.SMEM(rcv_taper.shape, F32),
            pltpu.VMEM(traces.shape, BF16),
            pltpu.SemaphoreType.DMA((3,)),
        ],
    )
    source_tables = call(
        functools.partial(source_tables_kernel, peers),
        (src_taper, *(jnp.transpose(v[:, 0], (0, 2, 1)) for v in (src_delay, src_frac))),
        [HBM, VMEM, VMEM],
        (
            shape((2, peers, half_peers, per_peer, LANES), I32),
            shape((2, peers, 4 * per_peer, half_peers * per_peer), BF16),
        ),
        [pltpu.SMEM(src_taper.shape, F32), pltpu.SemaphoreType.DMA],
    )

    def receivers(far):
        return call(
            functools.partial(receiver_kernel, far, peers),
            (other, place, weight, filt, band),
            [VMEM] * 5,
            shape((half_peers, per_peer, time), BF16),
            [pltpu.VMEM((blocks, rows // 2 + 2 * EDGE, LANES), F32)],
        )

    def sources(far, ins, partial=()):
        return call(
            functools.partial(source_kernel, far, peers),
            (*source_tables, band, *ins, *partial),
            [VMEM] * (3 + len(ins) + len(partial)),
            shape((peers, per_peer, time), BF16 if far else F32),
            [pltpu.VMEM((half_peers, blocks, per_peer, LANES), F32)],
        )

    far_out = receivers(1)
    far_in = [swap(far_out[r], r + half_peers, peers) for r in range(half_peers)]
    near_out = receivers(0)
    near_in = [near_out[0]] + [swap(near_out[r], r, peers) for r in range(1, half_peers)]
    partial = sources(0, near_in)
    result = sources(1, far_in, (partial,))
    return result.reshape(peers, 1, per_peer, time)


def swap(block, step, peers):
    return lax.ppermute(block, "shot", [(i, i ^ step) for i in range(peers)])


def solution(mesh):
    return jax.shard_map(
        body,
        mesh=mesh,
        in_specs=(
            P(("slab", "shot"), "rcv", None),
            P(("slab", "shot"), "rcv", None),
            P(("slab", "shot"), "rcv", None),
            P(("slab", "shot")),
            P("slab", "rcv", "shot", None),
            P("slab", "rcv", "shot", None),
            P(),
            P(),
        ),
        out_specs=P("slab", "rcv", "shot", None),
        check_vma=False,
    )
```

```python
import functools
import math

import jax
import jax.numpy as jnp
from jax import lax
from jax.experimental import pallas as pl
from jax.experimental.pallas import tpu as pltpu
from jax.sharding import PartitionSpec as P


AR = 4
AS = 4
TRI = 2
KR = 9
KS = 9
LANES = 128
SUB = 8
EDGE = 16
F32 = jnp.float32
BF16 = jnp.bfloat16
I32 = jnp.int32
GRANT = 24 << 20
LIVE = 2 * KR
TAPER = LIVE + 1
SOURCE_TAPER = TAPER + 1


def iota(shape, axis):
    return lax.broadcasted_iota(I32, shape, axis)


def filter_band(width):
    height = width + 2 * LANES
    away = jnp.abs(iota((height, width), 1) - (iota((height, width), 0) - LANES))
    energy = float(sum((TRI - abs(m)) ** 2 for m in range(1 - TRI, TRI)))
    return (jnp.maximum(TRI - away, 0).astype(F32) / math.sqrt(energy)).astype(BF16)


def pair_of(blocks):
    return 2 if blocks % 2 == 0 else 1


def filtered(source, band, store):
    blocks = source.shape[1] // LANES
    step = pair_of(blocks)
    for b in range(0, blocks, step):
        low, high = max(b - 1, 0), min(b + step + 1, blocks)
        start = (low - b + 1) * LANES
        part = source[:, low * LANES : high * LANES]
        dot = jnp.dot(part, band[start : start + (high - low) * LANES, :], preferred_element_type=F32)
        value = dot.astype(BF16).astype(F32)
        for i in range(step):
            store(b + i, value[:, i * LANES : (i + 1) * LANES])


def filtered_few(source, band):
    rows, time = source.shape
    blank = jnp.zeros((rows, LANES), BF16)
    wide = jnp.concatenate([blank, source, blank], axis=1)
    stack = jnp.concatenate([wide[:, t : t + 3 * LANES] for t in range(0, time, LANES)], axis=0)
    dot = jnp.dot(stack, band[: 3 * LANES, :LANES], preferred_element_type=F32).astype(BF16).astype(F32)
    return [dot[i : i + rows] for i in range(0, dot.shape[0], rows)]


def spread(table, pick):
    dims = (((0,), (0,)), ((), ()))
    return lax.dot_general(table.astype(F32).astype(BF16), pick.astype(BF16), dims, preferred_element_type=F32)


def weight_parts(frac, taper, keep):
    two = jnp.where(keep, frac * (taper * (1.0 / 256.0)), 0.0)
    one = jnp.where(keep, taper, 0.0) - two
    parts = []
    for value in (one, two):
        high = value.astype(BF16).astype(F32)
        parts += [high, value - high]
    return parts


def shifted(load, place, blocks):
    index = place & (LANES - 1)
    here = place < LANES
    moved = [jnp.take_along_axis(load(b), index, axis=1, mode="promise_in_bounds") for b in range(blocks)]
    moved.append(jnp.zeros_like(moved[0]))
    return [jnp.where(here, moved[b], moved[b + 1]) for b in range(blocks)]


def weighted(weights, taps, blocks, rows, lane):
    first, second = [], []
    step = pair_of(blocks)
    for b in range(0, blocks, step):
        stack = jnp.concatenate(
            [jnp.concatenate([tap[b + i] for tap in taps], axis=0).astype(BF16) for i in range(step)], axis=1
        )
        dot = jnp.dot(weights, stack, preferred_element_type=F32)
        for i in range(step):
            cols = slice(i * LANES, (i + 1) * LANES)
            first.append(dot[:rows, cols] + dot[rows : 2 * rows, cols])
            second.append(dot[2 * rows : 3 * rows, cols] + dot[3 * rows :, cols])
    rolled = [pltpu.roll(v, LANES - 1, 1) for v in second] + [jnp.zeros_like(second[0])]
    inner = lane < LANES - 1
    return [first[b] + jnp.where(inner, rolled[b], rolled[b + 1]) for b in range(blocks)]


def lookup(row, index):
    wide = jnp.broadcast_to(row, (SUB, LANES))
    return jnp.take_along_axis(wide, index[:SUB], axis=1, mode="promise_in_bounds")[:1]


def receiver_tables_kernel(small_ref, place_ref, weight_ref, band_ref):
    rows = small_ref.shape[1]
    delay, frac = small_ref[:KR, :], small_ref[KR : 2 * KR, :]
    band_ref[...] = filter_band(band_ref.shape[1])
    for a in range(KR):
        pick = iota((KR, LANES), 0) == a
        place_ref[a] = iota((rows, LANES), 1) + spread(delay, pick).astype(I32)
    wide = (rows, LANES)
    tap = iota((KR, LANES), 1) // SUB == iota((KR, LANES), 0)
    row, lane = iota(wide, 0), iota(wide, 1)
    line = row + lax.axis_index("rcv") * rows
    live = jnp.minimum(small_ref[LIVE : LIVE + 1, :LANES].astype(I32), rows * lax.axis_size("rcv"))
    source = line + lane // SUB - AR
    keep = (lane % SUB == row % SUB) & (lane < KR * SUB) & (source >= 0) & (source < live)
    fold = jnp.minimum(line + AR, live - 1) - jnp.maximum(line - AR, 0) + 1
    taper = lookup(small_ref[TAPER : TAPER + 1, :LANES], lane // SUB)
    taper = taper / jnp.sqrt(jnp.maximum(fold, 1).astype(F32))
    for i, part in enumerate(weight_parts(spread(frac, tap), taper, keep)):
        weight_ref[i] = part


def filter_kernel(traces_ref, band_ref, filt_ref):
    def store(b, value):
        filt_ref[b] = value

    filtered(traces_ref[...], band_ref, store)


def receiver_kernel(far, peers, other_ref, place_ref, weight_ref, filt_ref, band_ref, out_ref, src_ref):
    blocks, rows = filt_ref.shape[:2]
    part = rows // 2
    per_peer = rows // peers
    me = lax.axis_index("shot")
    mine = me // (peers // 2)
    half = (1 - mine) if far else mine
    low = me % (peers // 2)
    base = pl.multiple_of(half * part, part)

    left_at = pl.ds(pl.multiple_of(jnp.maximum(base - EDGE, 0), EDGE), EDGE)
    right_at = pl.ds(pl.multiple_of(jnp.minimum(base + part, rows - EDGE), EDGE), EDGE)
    far_side = pl.multiple_of(jnp.where(half == 0, rows - EDGE, 0), EDGE)
    other = filtered_few(other_ref[pl.ds(far_side, EDGE), :], band_ref)
    for b in range(blocks):
        src_ref[b, :EDGE] = jnp.where(half == 0, other[b], filt_ref[b, left_at, :])
        src_ref[b, EDGE : EDGE + part] = filt_ref[b, pl.ds(base, part), :]
        src_ref[b, EDGE + part :] = jnp.where(half == 1, other[b], filt_ref[b, right_at, :])

    lane = iota((SUB, LANES), 1)
    totals = []
    for g in range(part // SUB):
        at = pl.ds(pl.multiple_of(base + g * SUB, SUB), SUB)
        taps = []
        for a in range(KR):
            row = EDGE + g * SUB + a - AR
            taps.append(shifted(lambda b: src_ref[b, row : row + SUB, :], place_ref[a, at, :], blocks))
        weights = jnp.concatenate([weight_ref[i, at, : KR * SUB] for i in range(4)], axis=0).astype(BF16)
        totals.append(weighted(weights, taps, blocks, SUB, lane))
        step = max(1, min(2, per_peer // SUB))
        if len(totals) < step:
            continue
        first = (g + 1 - step) * SUB
        for s in range(0, step * SUB, min(step * SUB, per_peer)):
            height = min(step * SUB, per_peer)
            peer = ((first + s) // per_peer) ^ low
            start = (first + s) % per_peer
            for b in range(blocks):
                value = jnp.concatenate([t[b] for t in totals], axis=0).astype(BF16)
                out_ref[peer, start : start + height, b * LANES : (b + 1) * LANES] = value[s : s + height]
        totals = []


def source_tables_kernel(peers, share, small_ref, table_ref, place_ref, weight_ref):
    rows = table_ref.shape[2]
    wide = share * rows
    for k in range(peers):
        delay, frac = table_ref[k, :KS], table_ref[k, KS:]
        count = min(k + AS, peers - 1) - max(k - AS, 0) + 1
        for p in range(peers):
            place = iota((rows, LANES), 1)
            if abs(p - k) <= AS:
                place = place + spread(delay, iota((KS, LANES), 0) == p - k + AS).astype(I32)
            place_ref[k, p] = place
        row, lane = iota((rows, LANES), 0), iota((rows, LANES), 1)
        for q in range(peers // share):
            tap = AS + q * share + lane // rows - k
            keep = (lane % rows == row) & (tap >= 0) & (tap < KS) & (lane < wide)
            index = jnp.clip(AS + q * share + iota((SUB, LANES), 1) // rows - k, 0, KS - 1)
            taper = lookup(small_ref[SOURCE_TAPER : SOURCE_TAPER + 1, :LANES], index) * (1.0 / math.sqrt(count))
            column = AS + q * share + iota((KS, LANES), 1) // rows - k
            parts = weight_parts(spread(frac, column == iota((KS, LANES), 0)), taper, keep)
            weight_ref[k, q] = jnp.concatenate(parts, axis=0).astype(BF16)[:, :wide]


def source_kernel(call_index, last, peers, share, place_ref, weight_ref, band_ref, *refs):
    ins, refs = refs[:share], refs[share:]
    if call_index:
        part_ref, refs = refs[0], refs[1:]
    if last:
        out_ref, src_ref, done_ref, sem = refs
    else:
        out_ref, src_ref = refs
    per_peer, time = ins[0].shape
    blocks = time // LANES
    me = lax.axis_index("shot")
    group = (me // share) ^ call_index
    slots = [(me % share) ^ i for i in range(share)]

    def store(b, value):
        for i in range(share):
            src_ref[slots[i], b] = value[i * per_peer : (i + 1) * per_peer]

    filtered(jnp.concatenate([ref[...] for ref in ins], axis=0), band_ref, store)
    rows = min(SUB, per_peer)
    lane = iota((per_peer, LANES), 1)
    copies = []
    for k in range(peers):
        taps = []
        for e in range(share):
            for i in range(0, per_peer, rows):
                at = slice(i, i + rows)
                place = place_ref[k, group * share + e, at, :]
                taps.append(shifted(lambda b: src_ref[e, b, at, :], place, blocks))
        total = weighted(weight_ref[k, group], taps, blocks, per_peer, lane)
        target = done_ref if last else out_ref
        for b in range(blocks):
            cols = slice(b * LANES, (b + 1) * LANES)
            value = total[b]
            if call_index:
                value = value + part_ref[k, :, cols]
            target[k, :, cols] = value.astype(target.dtype)
        if last:
            copies.append(pltpu.make_async_copy(done_ref.at[k], out_ref.at[k], sem.at[k]))
            copies[-1].start()
    for copy in copies:
        copy.wait()


VMEM = pl.BlockSpec(memory_space=pltpu.VMEM)
ANY = pl.BlockSpec(memory_space=pl.ANY)


def call(kernel, args, outs, scratch=(), cost=0, out_specs=None):
    return pl.pallas_call(
        kernel,
        out_shape=outs,
        in_specs=[VMEM] * len(args),
        out_specs=out_specs or ([VMEM] * len(outs) if isinstance(outs, tuple) else VMEM),
        scratch_shapes=list(scratch),
        compiler_params=pltpu.CompilerParams(vmem_limit_bytes=GRANT),
        cost_estimate=pl.CostEstimate(flops=cost, bytes_accessed=0, transcendentals=0) if cost else None,
    )(*args)


def body(traces, rcv_delay, rcv_frac, live_count, src_delay, src_frac, rcv_taper, src_taper):
    rows, time = traces.shape[1:]
    blocks = time // LANES
    peers = lax.axis_size("shot")
    half_peers = peers // 2
    per_peer = rows // peers
    traces = traces[0]
    other = lax.ppermute(traces, "rcv", [(0, 1), (1, 0)])
    shape = jax.ShapeDtypeStruct
    width = pair_of(blocks) * LANES

    share = max(1, peers // 4)
    lanes = max(rows, LANES)
    small = jnp.concatenate(
        [
            jnp.pad(rcv_delay[0].T.astype(F32), ((0, 0), (0, lanes - rows))),
            jnp.pad(rcv_frac[0].T.astype(F32), ((0, 0), (0, lanes - rows))),
            jnp.broadcast_to(live_count.astype(F32)[:, None], (1, lanes)),
            jnp.pad(rcv_taper[None], ((0, 0), (0, lanes - KR))),
            jnp.pad(src_taper[None], ((0, 0), (0, lanes - KS))),
        ],
        axis=0,
    )
    place, weight, band = call(
        receiver_tables_kernel,
        (small,),
        (
            shape((KR, rows, LANES), I32),
            shape((4, rows, LANES), F32),
            shape((width + 2 * LANES, width), BF16),
        ),
        cost=2_000_000_000,
    )
    filt = call(filter_kernel, (traces, band), shape((blocks, rows, LANES), F32))

    def receivers(far):
        return call(
            functools.partial(receiver_kernel, far, peers),
            (other, place, weight, filt, band),
            shape((half_peers, per_peer, time), BF16),
            [pltpu.VMEM((blocks, rows // 2 + 2 * EDGE, LANES), F32)],
        )

    far_out = receivers(1)
    far_in = [swap(far_out[r], r + half_peers, peers) for r in range(half_peers)]
    near_out = receivers(0)
    near_in = [near_out[0]] + [swap(near_out[r], r, peers) for r in range(1, half_peers)]

    table = jnp.concatenate([jnp.transpose(v[:, 0], (0, 2, 1)).astype(F32) for v in (src_delay, src_frac)], axis=1)
    source_tables = call(
        functools.partial(source_tables_kernel, peers, share),
        (small, table),
        (
            shape((peers, peers, per_peer, LANES), I32),
            shape((peers, peers // share, 4 * per_peer, share * per_peer), BF16),
        ),
    )
    arrived = near_in + far_in
    result = None
    turns = range(peers // share)
    for turn in turns:
        last = turn == turns[-1]
        extra = [] if turn == 0 else [result]
        scratch = [pltpu.VMEM((share, blocks, per_peer, LANES), F32)]
        if last:
            scratch += [pltpu.VMEM((peers, per_peer, time), BF16), pltpu.SemaphoreType.DMA((peers,))]
        result = call(
            functools.partial(source_kernel, turn, last, peers, share),
            (*source_tables, band, *arrived[turn * share : (turn + 1) * share], *extra),
            shape((peers, per_peer, time), BF16 if last else F32),
            scratch,
            out_specs=ANY if last else VMEM,
        )
    return result.reshape(peers, 1, per_peer, time)


def swap(block, step, peers):
    return lax.ppermute(block, "shot", [(i, i ^ step) for i in range(peers)])


def solution(mesh):
    return jax.shard_map(
        body,
        mesh=mesh,
        in_specs=(
            P(("slab", "shot"), "rcv", None),
            P(("slab", "shot"), "rcv", None),
            P(("slab", "shot"), "rcv", None),
            P(("slab", "shot")),
            P("slab", "rcv", "shot", None),
            P("slab", "rcv", "shot", None),
            P(),
            P(),
        ),
        out_specs=P("slab", "rcv", "shot", None),
        check_vma=False,
    )
```

```python
import functools
import math

import jax
import jax.numpy as jnp
from jax import lax
from jax.experimental import pallas as pl
from jax.experimental.pallas import tpu as pltpu
from jax.sharding import PartitionSpec as P


AR = 4
AS = 4
TRI = 2
KR = 9
KS = 9
LANES = 128
SUB = 8
EDGE = 16
F32 = jnp.float32
BF16 = jnp.bfloat16
I32 = jnp.int32
GRANT = 24 << 20


def iota(shape, axis):
    return lax.broadcasted_iota(I32, shape, axis)


def filter_band(width):
    height = width + 2 * LANES
    away = jnp.abs(iota((height, width), 1) - (iota((height, width), 0) - LANES))
    energy = float(sum((TRI - abs(m)) ** 2 for m in range(1 - TRI, TRI)))
    return (jnp.maximum(TRI - away, 0).astype(F32) / math.sqrt(energy)).astype(BF16)


def pair_of(blocks):
    return 2 if blocks % 2 == 0 else 1


def filtered(source, band, store):
    blocks = source.shape[1] // LANES
    step = pair_of(blocks)
    for b in range(0, blocks, step):
        low, high = max(b - 1, 0), min(b + step + 1, blocks)
        start = (low - b + 1) * LANES
        part = source[:, low * LANES : high * LANES]
        dot = jnp.dot(part, band[start : start + (high - low) * LANES, :], preferred_element_type=F32)
        value = dot.astype(BF16).astype(F32)
        for i in range(step):
            store(b + i, value[:, i * LANES : (i + 1) * LANES])


def filtered_few(source, band):
    rows, time = source.shape
    blank = jnp.zeros((rows, LANES), BF16)
    wide = jnp.concatenate([blank, source, blank], axis=1)
    stack = jnp.concatenate([wide[:, t : t + 3 * LANES] for t in range(0, time, LANES)], axis=0)
    dot = jnp.dot(stack, band[: 3 * LANES, :LANES], preferred_element_type=F32).astype(BF16).astype(F32)
    return [dot[i : i + rows] for i in range(0, dot.shape[0], rows)]


def spread(table, pick):
    dims = (((0,), (0,)), ((), ()))
    return lax.dot_general(table.astype(F32).astype(BF16), pick.astype(BF16), dims, preferred_element_type=F32)


def weight_parts(frac, taper, keep):
    two = jnp.where(keep, frac * (taper * (1.0 / 256.0)), 0.0)
    one = jnp.where(keep, taper, 0.0) - two
    parts = []
    for value in (one, two):
        high = value.astype(BF16).astype(F32)
        parts += [high, value - high]
    return parts


def shifted(load, place, blocks):
    index = place & (LANES - 1)
    here = place < LANES
    moved = [jnp.take_along_axis(load(b), index, axis=1, mode="promise_in_bounds") for b in range(blocks)]
    moved.append(jnp.zeros_like(moved[0]))
    return [jnp.where(here, moved[b], moved[b + 1]) for b in range(blocks)]


def sums(weights, taps, blocks, rows):
    first, second = [], []
    step = pair_of(blocks)
    for b in range(0, blocks, step):
        stack = jnp.concatenate(
            [jnp.concatenate([tap[b + i] for tap in taps], axis=0).astype(BF16) for i in range(step)], axis=1
        )
        dot = jnp.dot(weights, stack, preferred_element_type=F32)
        for i in range(step):
            cols = slice(i * LANES, (i + 1) * LANES)
            first.append(dot[:rows, cols] + dot[rows : 2 * rows, cols])
            second.append(dot[2 * rows : 3 * rows, cols] + dot[3 * rows :, cols])
    return first, second


def join(first, second):
    rolled = [pltpu.roll(v, LANES - 1, 1) for v in second] + [jnp.zeros_like(second[0])]
    inner = iota(second[0].shape, 1) < LANES - 1
    return [v + jnp.where(inner, rolled[b], rolled[b + 1]) for b, v in enumerate(first)]


def chosen(taper_ref, tap):
    value = jnp.zeros(tap.shape, F32)
    for a in range(taper_ref.shape[0]):
        value = jnp.where(tap == a, taper_ref[a], value)
    return value


def head_kernel(
    live_ref, taper_in, delay_in, frac_in, traces_in, place_ref, weight_ref, filt_ref, band_ref,
    taper_ref, delay_ref, frac_ref, traces_ref, sem,
):
    sources = (delay_in, frac_in, taper_in, traces_in)
    targets = (delay_ref, frac_ref, taper_ref, traces_ref)
    copies = [pltpu.make_async_copy(s, t, sem.at[i]) for i, (s, t) in enumerate(zip(sources, targets))]
    for copy in copies:
        copy.start()
    band_ref[...] = filter_band(band_ref.shape[1])
    for copy in copies[:3]:
        copy.wait()
    rows = delay_ref.shape[2]
    delay, frac = delay_ref[:, 0, :], frac_ref[:, 0, :]
    for a in range(KR):
        pick = iota((KR, LANES), 0) == a
        place_ref[a] = iota((rows, LANES), 1) + spread(delay, pick).astype(I32)
    wide = (rows, LANES)
    tap = iota((KR, LANES), 1) // SUB == iota((KR, LANES), 0)
    row, lane = iota(wide, 0), iota(wide, 1)
    line = row + lax.axis_index("rcv") * rows
    live = jnp.minimum(live_ref[0], rows * lax.axis_size("rcv"))
    source = line + lane // SUB - AR
    keep = (lane % SUB == row % SUB) & (lane < KR * SUB) & (source >= 0) & (source < live)
    fold = jnp.minimum(line + AR, live - 1) - jnp.maximum(line - AR, 0) + 1
    taper = chosen(taper_ref, iota((1, LANES), 1) // SUB)
    taper = taper / jnp.sqrt(jnp.maximum(fold, 1).astype(F32))
    for i, part in enumerate(weight_parts(spread(frac, tap), taper, keep)):
        weight_ref[i] = part

    def store(b, value):
        filt_ref[b] = value

    copies[3].wait()
    filtered(traces_ref[...], band_ref, store)


def receiver_kernel(far, peers, other_ref, place_ref, weight_ref, filt_ref, band_ref, out_ref, src_ref):
    blocks, rows = filt_ref.shape[:2]
    part = rows // 2
    per_peer = rows // peers
    me = lax.axis_index("shot")
    mine = me // (peers // 2)
    half = (1 - mine) if far else mine
    low = me % (peers // 2)
    base = pl.multiple_of(half * part, part)

    left_at = pl.ds(pl.multiple_of(jnp.maximum(base - EDGE, 0), EDGE), EDGE)
    right_at = pl.ds(pl.multiple_of(jnp.minimum(base + part, rows - EDGE), EDGE), EDGE)
    far_side = pl.multiple_of(jnp.where(half == 0, rows - EDGE, 0), EDGE)
    other = filtered_few(other_ref[pl.ds(far_side, EDGE), :], band_ref)
    for b in range(blocks):
        src_ref[b, :EDGE] = jnp.where(half == 0, other[b], filt_ref[b, left_at, :])
        src_ref[b, EDGE : EDGE + part] = filt_ref[b, pl.ds(base, part), :]
        src_ref[b, EDGE + part :] = jnp.where(half == 1, other[b], filt_ref[b, right_at, :])

    step = max(1, min(2, per_peer // SUB))
    count = part // (step * SUB)
    for c in range(count):
        totals = []
        for g in range(c * step, (c + 1) * step):
            at = pl.ds(pl.multiple_of(base + g * SUB, SUB), SUB)
            taps = []
            for a in range(KR):
                row = EDGE + g * SUB + a - AR
                taps.append(shifted(lambda b: src_ref[b, row : row + SUB, :], place_ref[a, at, :], blocks))
            weights = jnp.concatenate([weight_ref[i, at, : KR * SUB] for i in range(4)], axis=0).astype(BF16)
            totals.append(join(*sums(weights, taps, blocks, SUB)))
        first = c * step * SUB
        height = min(step * SUB, per_peer)
        for s in range(0, step * SUB, height):
            peer = ((first + s) // per_peer) ^ low
            start = (first + s) % per_peer
            for b in range(blocks):
                value = jnp.concatenate([t[b] for t in totals], axis=0).astype(BF16)
                out_ref[peer, start : start + height, b * LANES : (b + 1) * LANES] = value[s : s + height]


def source_tables_kernel(peers, share, calls, taper_in, delay_ref, frac_ref, place_ref, weight_ref, taper_ref, sem):
    rows = delay_ref.shape[2]
    me = lax.axis_index("shot")
    wide = share * rows
    copy = pltpu.make_async_copy(taper_in, taper_ref, sem)
    copy.start()
    copy.wait()

    def shot_of(groups, lane):
        shot = jnp.zeros_like(lane)
        for i, group in enumerate(groups):
            shot = jnp.where(lane // wide == i, ((me // share) ^ group) * share + (lane % wide) // rows, shot)
        return shot

    for k in range(peers):
        delay, frac = delay_ref[k], frac_ref[k]
        scale = 1.0 / math.sqrt(min(k + AS, peers - 1) - max(k - AS, 0) + 1)
        for p in range(peers):
            place = iota((rows, LANES), 1)
            if abs(p - k) <= AS:
                place = place + spread(delay, iota((KS, LANES), 0) == p - k + AS).astype(I32)
            place_ref[k, p] = place
        row, lane = iota((rows, LANES), 0), iota((rows, LANES), 1)
        for c, groups in enumerate(calls):
            used = len(groups) * wide
            tap = shot_of(groups, lane) - k + AS
            keep = (lane % rows == row) & (tap >= 0) & (tap < KS) & (lane < used)
            taper = chosen(taper_ref, shot_of(groups, iota((1, LANES), 1)) - k + AS)
            column = shot_of(groups, iota((KS, LANES), 1)) - k + AS
            parts = weight_parts(
                spread(frac, column == iota((KS, LANES), 0)), taper * scale, keep
            )
            weight_ref[c, k] = jnp.concatenate(parts, axis=0).astype(BF16)[:, :used]


def source_kernel(turn, last, peers, share, groups, place_ref, weight_ref, band_ref, *refs):
    used = len(groups) * share
    ins, refs = refs[:used], refs[used:]
    if turn:
        part_ref, refs = refs[0], refs[1:]
    if last:
        out_ref, src_ref, done_ref, sem = refs
    else:
        out_ref, src_ref = refs
    per_peer, time = ins[0].shape
    blocks = time // LANES
    me = lax.axis_index("shot")
    shots = [((me // share) ^ group) * share + e for group in groups for e in range(share)]
    slots = [i * share + ((me % share) ^ e) for i in range(len(groups)) for e in range(share)]

    def store(b, value):
        for i in range(used):
            src_ref[slots[i], b] = value[i * per_peer : (i + 1) * per_peer]

    filtered(jnp.concatenate([ref[...] for ref in ins], axis=0), band_ref, store)
    rows = min(SUB, per_peer)
    copies = []
    for k in range(peers):
        taps = []
        for i in range(used):
            for r in range(0, per_peer, rows):
                at = slice(r, r + rows)
                taps.append(shifted(lambda b: src_ref[i, b, at, :], place_ref[k, shots[i], at, :], blocks))
        pair = sums(weight_ref[turn, k], taps, blocks, per_peer)
        if turn:
            pair = [
                [v + part_ref[i, k, :, b * LANES : (b + 1) * LANES] for b, v in enumerate(part)]
                for i, part in enumerate(pair)
            ]
        if last:
            for b, value in enumerate(join(*pair)):
                done_ref[k, :, b * LANES : (b + 1) * LANES] = value.astype(BF16)
            copies.append(pltpu.make_async_copy(done_ref.at[k], out_ref.at[k], sem.at[k]))
            copies[-1].start()
        else:
            for i, part in enumerate(pair):
                for b, value in enumerate(part):
                    out_ref[i, k, :, b * LANES : (b + 1) * LANES] = value
    for copy in copies:
        copy.wait()


VMEM = pl.BlockSpec(memory_space=pltpu.VMEM)
SMEM = pl.BlockSpec(memory_space=pltpu.SMEM)
ANY = pl.BlockSpec(memory_space=pl.ANY)


def stay(value):
    return pltpu.with_memory_space_constraint(value, pltpu.HBM)


def call(kernel, args, outs, scratch=(), in_specs=None, out_specs=None):
    return pl.pallas_call(
        kernel,
        out_shape=outs,
        in_specs=in_specs or [VMEM] * len(args),
        out_specs=out_specs or ([VMEM] * len(outs) if isinstance(outs, tuple) else VMEM),
        scratch_shapes=list(scratch),
        compiler_params=pltpu.CompilerParams(vmem_limit_bytes=GRANT),
    )(*args)


def body(traces, rcv_delay, rcv_frac, live_count, src_delay, src_frac, rcv_taper, src_taper):
    rows, time = traces.shape[1:]
    blocks = time // LANES
    peers = lax.axis_size("shot")
    half_peers = peers // 2
    per_peer = rows // peers
    traces = traces[0]
    other = lax.ppermute(traces, "rcv", [(0, 1), (1, 0)])
    shape = jax.ShapeDtypeStruct
    width = pair_of(blocks) * LANES

    share = max(1, peers // 4)
    groups = list(range(peers // share))
    calls = [g for g in (groups[0::2], groups[1::2]) if g]
    delay, frac = (jnp.transpose(v, (2, 0, 1)) for v in (rcv_delay, rcv_frac))
    place, weight, filt, band = call(
        head_kernel,
        [live_count, *(stay(v) for v in (rcv_taper, delay, frac, traces))],
        (
            shape((KR, rows, LANES), I32),
            shape((4, rows, LANES), F32),
            shape((blocks, rows, LANES), F32),
            shape((width + 2 * LANES, width), BF16),
        ),
        [
            pltpu.SMEM(rcv_taper.shape, F32),
            pltpu.VMEM(delay.shape, I32),
            pltpu.VMEM(frac.shape, I32),
            pltpu.VMEM(traces.shape, BF16),
            pltpu.SemaphoreType.DMA((4,)),
        ],
        in_specs=[SMEM] + [ANY] * 4,
    )

    def receivers(far):
        return call(
            functools.partial(receiver_kernel, far, peers),
            (other, place, weight, filt, band),
            shape((half_peers, per_peer, time), BF16),
            [pltpu.VMEM((blocks, rows // 2 + 2 * EDGE, LANES), F32)],
        )

    far_out = receivers(1)
    far_in = [swap(far_out[r], r + half_peers, peers) for r in range(half_peers)]
    near_out = receivers(0)
    near_in = [near_out[0]] + [swap(near_out[r], r, peers) for r in range(1, half_peers)]

    tables = [jnp.transpose(v[:, 0], (0, 2, 1)) for v in (src_delay, src_frac)]
    source_tables = call(
        functools.partial(source_tables_kernel, peers, share, calls),
        (stay(src_taper), *tables),
        (
            shape((peers, peers, per_peer, LANES), I32),
            shape((len(calls), peers, 4 * per_peer, len(calls[0]) * share * per_peer), BF16),
        ),
        [pltpu.SMEM(src_taper.shape, F32), pltpu.SemaphoreType.DMA],
        in_specs=[ANY, VMEM, VMEM],
    )
    arrived = near_in + far_in
    result = None
    for turn, groups in enumerate(calls):
        last = turn == len(calls) - 1
        extra = [] if turn == 0 else [result]
        ins = [arrived[g * share + e] for g in groups for e in range(share)]
        scratch = [pltpu.VMEM((len(ins), blocks, per_peer, LANES), F32)]
        if last:
            scratch += [pltpu.VMEM((peers, per_peer, time), BF16), pltpu.SemaphoreType.DMA((peers,))]
        result = call(
            functools.partial(source_kernel, turn, last, peers, share, groups),
            (*source_tables, band, *ins, *extra),
            shape((peers, per_peer, time), BF16) if last else shape((2, peers, per_peer, time), F32),
            scratch,
            out_specs=ANY if last else VMEM,
        )
    return result.reshape(peers, 1, per_peer, time)


def swap(block, step, peers):
    return lax.ppermute(block, "shot", [(i, i ^ step) for i in range(peers)])


def solution(mesh):
    return jax.shard_map(
        body,
        mesh=mesh,
        in_specs=(
            P(("slab", "shot"), "rcv", None),
            P(("slab", "shot"), "rcv", None),
            P(("slab", "shot"), "rcv", None),
            P(("slab", "shot")),
            P("slab", "rcv", "shot", None),
            P("slab", "rcv", "shot", None),
            P(),
            P(),
        ),
        out_specs=P("slab", "rcv", "shot", None),
        check_vma=False,
    )
```

```python
import functools
import math

import jax
import jax.numpy as jnp
from jax import lax
from jax.experimental import pallas as pl
from jax.experimental.pallas import tpu as pltpu
from jax.sharding import PartitionSpec as P


AR = 4
AS = 4
TRI = 2
KR = 9
KS = 9
LANES = 128
SUB = 8
EDGE = 16
PIECES = 4
F32 = jnp.float32
BF16 = jnp.bfloat16
I32 = jnp.int32
GRANT = 24 << 20


def iota(shape, axis):
    return lax.broadcasted_iota(I32, shape, axis)


def filter_band(width):
    size = (3 * LANES, LANES)
    away = jnp.abs(iota(size, 1) - (iota(size, 0) - LANES))
    energy = float(sum((TRI - abs(m)) ** 2 for m in range(1 - TRI, TRI)))
    one = (jnp.maximum(TRI - away, 0).astype(F32) / math.sqrt(energy)).astype(BF16)
    blank = jnp.zeros((LANES, LANES), BF16)
    count = width // LANES
    columns = [jnp.concatenate([blank] * i + [one] + [blank] * (count - 1 - i), axis=0) for i in range(count)]
    return jnp.concatenate(columns, axis=1)


def pair_of(blocks):
    return 2 if blocks % 2 == 0 else 1


def filtered(source, band, store):
    rows, time = source.shape
    high, wide = band.shape
    blank = jnp.zeros((rows, LANES), BF16)
    padded = jnp.concatenate([blank, source, blank], axis=1)
    stack = jnp.concatenate([padded[:, t : t + high] for t in range(0, time, wide)], axis=0)
    dot = jnp.dot(stack, band[...], preferred_element_type=F32).astype(BF16).astype(F32)
    for i, t in enumerate(range(0, time, wide)):
        for j in range(0, wide, LANES):
            store((t + j) // LANES, dot[i * rows : (i + 1) * rows, j : j + LANES])


def filtered_few(source, band):
    rows, time = source.shape
    blank = jnp.zeros((rows, LANES), BF16)
    wide = jnp.concatenate([blank, source, blank], axis=1)
    stack = jnp.concatenate([wide[:, t : t + 3 * LANES] for t in range(0, time, LANES)], axis=0)
    dot = jnp.dot(stack, band[: 3 * LANES, :LANES], preferred_element_type=F32).astype(BF16).astype(F32)
    return [dot[i : i + rows] for i in range(0, dot.shape[0], rows)]


def spread(table, pick):
    dims = (((0,), (0,)), ((), ()))
    return lax.dot_general(table.astype(F32).astype(BF16), pick.astype(BF16), dims, preferred_element_type=F32)


def weight_parts(frac, taper, keep):
    two = jnp.where(keep, frac * (taper * (1.0 / 256.0)), 0.0)
    one = jnp.where(keep, taper, 0.0) - two
    parts = []
    for value in (one, two):
        high = value.astype(BF16).astype(F32)
        parts += [high, value - high]
    return parts


def shifted(load, place, blocks):
    index = place & (LANES - 1)
    here = place < LANES
    moved = [jnp.take_along_axis(load(b), index, axis=1, mode="promise_in_bounds") for b in range(blocks)]
    moved.append(jnp.zeros_like(moved[0]))
    return [jnp.where(here, moved[b], moved[b + 1]) for b in range(blocks)]


def sums(weights, taps, blocks, rows):
    first, second = [], []
    step = pair_of(blocks)
    for b in range(0, blocks, step):
        stack = jnp.concatenate(
            [jnp.concatenate([tap[b + i] for tap in taps], axis=0).astype(BF16) for i in range(step)], axis=1
        )
        dot = jnp.dot(weights, stack, preferred_element_type=F32)
        for i in range(step):
            cols = slice(i * LANES, (i + 1) * LANES)
            first.append(dot[:rows, cols] + dot[rows : 2 * rows, cols])
            second.append(dot[2 * rows : 3 * rows, cols] + dot[3 * rows :, cols])
    return first, second


def join(first, second):
    rolled = [pltpu.roll(v, LANES - 1, 1) for v in second] + [jnp.zeros_like(second[0])]
    inner = iota(second[0].shape, 1) < LANES - 1
    return [v + jnp.where(inner, rolled[b], rolled[b + 1]) for b, v in enumerate(first)]


def chosen(taper_ref, tap):
    value = jnp.zeros(tap.shape, F32)
    for a in range(taper_ref.shape[0]):
        value = jnp.where(tap == a, taper_ref[a], value)
    return value


def head_kernel(
    live_ref, taper_in, source_taper_in, delay_in, frac_in, traces_in,
    place_ref, weight_ref, filt_ref, band_ref, source_taper_out, taper_ref, source_taper_ref, delay_ref, frac_ref, traces_ref, sem,
):
    pairs = [(delay_in, delay_ref), (frac_in, frac_ref), (taper_in, taper_ref), (source_taper_in, source_taper_ref)]
    height = traces_in.shape[0] // PIECES
    for i in range(PIECES):
        at = pl.ds(i * height, height)
        pairs.append((traces_in.at[at], traces_ref.at[at]))
    copies = [pltpu.make_async_copy(s, t, sem.at[i]) for i, (s, t) in enumerate(pairs)]
    for copy in copies:
        copy.start()
    band_ref[...] = filter_band(band_ref.shape[1])
    for copy in copies[:4]:
        copy.wait()
    rows = delay_ref.shape[2]
    source_taper_out[...] = chosen(source_taper_ref, iota((SUB, LANES), 1))
    delay, frac = delay_ref[:, 0, :], frac_ref[:, 0, :]
    for a in range(KR):
        pick = iota((KR, LANES), 0) == a
        place_ref[a] = iota((rows, LANES), 1) + spread(delay, pick).astype(I32)
    wide = (rows, LANES)
    tap = iota((KR, LANES), 1) // SUB == iota((KR, LANES), 0)
    row, lane = iota(wide, 0), iota(wide, 1)
    line = row + lax.axis_index("rcv") * rows
    live = jnp.minimum(live_ref[0], rows * lax.axis_size("rcv"))
    source = line + lane // SUB - AR
    keep = (lane % SUB == row % SUB) & (lane < KR * SUB) & (source >= 0) & (source < live)
    place = iota((1, rows), 1) + lax.axis_index("rcv") * rows
    fold = jnp.minimum(place + AR, live - 1) - jnp.maximum(place - AR, 0) + 1
    rest = 1.0 / jnp.sqrt(jnp.maximum(fold, 1).astype(F32))
    scale = jnp.zeros(wide, F32)
    for _ in range(3):
        part = rest.astype(BF16).astype(F32)
        rest = rest - part
        scale = scale + spread(part, iota((1, LANES), 1) >= 0)
    taper = chosen(taper_ref, iota((1, LANES), 1) // SUB) * scale
    for i, part in enumerate(weight_parts(spread(frac, tap), taper, keep)):
        weight_ref[i] = part

    def store(b, value):
        filt_ref[b] = value

    for copy in copies[4:]:
        copy.wait()
    filtered(traces_ref[...], band_ref, store)


def receiver_kernel(far, peers, other_ref, place_ref, weight_ref, filt_ref, band_ref, out_ref, src_ref):
    blocks, rows = filt_ref.shape[:2]
    part = rows // 2
    per_peer = rows // peers
    me = lax.axis_index("shot")
    mine = me // (peers // 2)
    half = (1 - mine) if far else mine
    low = me % (peers // 2)
    base = pl.multiple_of(half * part, part)

    left_at = pl.ds(pl.multiple_of(jnp.maximum(base - EDGE, 0), EDGE), EDGE)
    right_at = pl.ds(pl.multiple_of(jnp.minimum(base + part, rows - EDGE), EDGE), EDGE)
    far_side = pl.multiple_of(jnp.where(half == 0, rows - EDGE, 0), EDGE)
    other = filtered_few(other_ref[pl.ds(far_side, EDGE), :], band_ref)
    for b in range(blocks):
        src_ref[b, :EDGE] = jnp.where(half == 0, other[b], filt_ref[b, left_at, :])
        src_ref[b, EDGE : EDGE + part] = filt_ref[b, pl.ds(base, part), :]
        src_ref[b, EDGE + part :] = jnp.where(half == 1, other[b], filt_ref[b, right_at, :])

    step = max(1, min(2, per_peer // SUB))
    count = part // (step * SUB)
    for c in range(count):
        totals = []
        for g in range(c * step, (c + 1) * step):
            at = pl.ds(pl.multiple_of(base + g * SUB, SUB), SUB)
            taps = []
            for a in range(KR):
                row = EDGE + g * SUB + a - AR
                taps.append(shifted(lambda b: src_ref[b, row : row + SUB, :], place_ref[a, at, :], blocks))
            weights = jnp.concatenate([weight_ref[i, at, : KR * SUB] for i in range(4)], axis=0).astype(BF16)
            totals.append(join(*sums(weights, taps, blocks, SUB)))
        first = c * step * SUB
        height = min(step * SUB, per_peer)
        for s in range(0, step * SUB, height):
            peer = ((first + s) // per_peer) ^ low
            start = (first + s) % per_peer
            for b in range(blocks):
                value = jnp.concatenate([t[b] for t in totals], axis=0).astype(BF16)
                out_ref[peer, start : start + height, b * LANES : (b + 1) * LANES] = value[s : s + height]


def source_tables_kernel(peers, share, calls, taper_ref, delay_ref, frac_ref, place_ref, weight_ref):
    rows = delay_ref.shape[2]
    me = lax.axis_index("shot")
    wide = share * rows
    for k in range(peers):
        for p in range(peers):
            place = iota((rows, LANES), 1)
            if abs(p - k) <= AS:
                place = place + spread(delay_ref[k], iota((KS, LANES), 0) == p - k + AS).astype(I32)
            place_ref[k, p] = place

    def shot_of(groups, lane):
        shot = jnp.zeros_like(lane)
        for i, group in enumerate(groups):
            shot = jnp.where(lane // wide == i, ((me // share) ^ group) * share + (lane % wide) // rows, shot)
        return shot

    for k in range(peers):
        frac = frac_ref[k]
        scale = 1.0 / math.sqrt(min(k + AS, peers - 1) - max(k - AS, 0) + 1)
        row, lane = iota((rows, LANES), 0), iota((rows, LANES), 1)
        for c, groups in enumerate(calls):
            used = len(groups) * wide
            tap = shot_of(groups, lane) - k + AS
            keep = (lane % rows == row) & (tap >= 0) & (tap < KS) & (lane < used)
            index = jnp.clip(shot_of(groups, iota((SUB, LANES), 1)) - k + AS, 0, KS - 1)
            taper = jnp.take_along_axis(taper_ref[...], index, axis=1, mode="promise_in_bounds")[:1]
            column = shot_of(groups, iota((KS, LANES), 1)) - k + AS
            parts = weight_parts(
                spread(frac, column == iota((KS, LANES), 0)), taper * scale, keep
            )
            weight_ref[c, k, :, :used] = jnp.concatenate(parts, axis=0).astype(BF16)[:, :used]


def source_kernel(turn, last, peers, share, groups, place_ref, weight_ref, band_ref, *refs):
    used = len(groups) * share
    ins, refs = refs[:used], refs[used:]
    if turn:
        part_ref, refs = refs[0], refs[1:]
    if last:
        out_ref, src_ref, done_ref, sem = refs
    else:
        out_ref, src_ref = refs
    per_peer, time = ins[0].shape
    blocks = time // LANES
    me = lax.axis_index("shot")
    shots = [((me // share) ^ group) * share + e for group in groups for e in range(share)]
    slots = [i * share + ((me % share) ^ e) for i in range(len(groups)) for e in range(share)]

    def store(b, value):
        for i in range(used):
            src_ref[slots[i], b] = value[i * per_peer : (i + 1) * per_peer]

    filtered(jnp.concatenate([ref[...] for ref in ins], axis=0), band_ref, store)
    rows = min(SUB, per_peer)
    copies = []
    for k in range(peers):
        taps = []
        for i in range(used):
            for r in range(0, per_peer, rows):
                at = slice(r, r + rows)
                taps.append(shifted(lambda b: src_ref[i, b, at, :], place_ref[k, shots[i], at, :], blocks))
        pair = sums(weight_ref[turn, k, :, : used * per_peer], taps, blocks, per_peer)
        if turn:
            pair = [
                [v + part_ref[i, k, :, b * LANES : (b + 1) * LANES] for b, v in enumerate(part)]
                for i, part in enumerate(pair)
            ]
        if last:
            for b, value in enumerate(join(*pair)):
                done_ref[k, :, b * LANES : (b + 1) * LANES] = value.astype(BF16)
            copies.append(pltpu.make_async_copy(done_ref.at[k], out_ref.at[k], sem.at[k]))
            copies[-1].start()
        else:
            for i, part in enumerate(pair):
                for b, value in enumerate(part):
                    out_ref[i, k, :, b * LANES : (b + 1) * LANES] = value
    for copy in copies:
        copy.wait()


VMEM = pl.BlockSpec(memory_space=pltpu.VMEM)
SMEM = pl.BlockSpec(memory_space=pltpu.SMEM)
ANY = pl.BlockSpec(memory_space=pl.ANY)


def stay(value):
    return pltpu.with_memory_space_constraint(value, pltpu.HBM)


def call(kernel, args, outs, scratch=(), in_specs=None, out_specs=None):
    return pl.pallas_call(
        kernel,
        out_shape=outs,
        in_specs=in_specs or [VMEM] * len(args),
        out_specs=out_specs or ([VMEM] * len(outs) if isinstance(outs, tuple) else VMEM),
        scratch_shapes=list(scratch),
        compiler_params=pltpu.CompilerParams(vmem_limit_bytes=GRANT),
    )(*args)


def body(traces, rcv_delay, rcv_frac, live_count, src_delay, src_frac, rcv_taper, src_taper):
    rows, time = traces.shape[1:]
    blocks = time // LANES
    peers = lax.axis_size("shot")
    half_peers = peers // 2
    per_peer = rows // peers
    traces = traces[0]
    other = lax.ppermute(traces, "rcv", [(0, 1), (1, 0)])
    shape = jax.ShapeDtypeStruct
    width = pair_of(blocks) * LANES

    share = 1
    groups = list(range(peers // share))
    cut = half_peers // 2
    early = groups[:cut] + groups[half_peers : half_peers + cut]
    late = groups[half_peers - 1 : half_peers]
    calls = [g for g in (early, [g for g in groups if g not in early + late], late) if g]
    delay, frac = (jnp.transpose(v, (2, 0, 1)) for v in (rcv_delay, rcv_frac))
    place, weight, filt, band, source_taper = call(
        head_kernel,
        [live_count, *(stay(v) for v in (rcv_taper, src_taper, delay, frac, traces))],
        (
            shape((KR, rows, LANES), I32),
            shape((4, rows, LANES), F32),
            shape((blocks, rows, LANES), F32),
            shape((width + 2 * LANES, width), BF16),
            shape((SUB, LANES), F32),
        ),
        [
            pltpu.SMEM(rcv_taper.shape, F32),
            pltpu.SMEM(src_taper.shape, F32),
            pltpu.VMEM(delay.shape, I32),
            pltpu.VMEM(frac.shape, I32),
            pltpu.VMEM(traces.shape, BF16),
            pltpu.SemaphoreType.DMA((4 + PIECES,)),
        ],
        in_specs=[SMEM] + [ANY] * 5,
    )

    def receivers(far):
        return call(
            functools.partial(receiver_kernel, far, peers),
            (other, place, weight, filt, band),
            shape((half_peers, per_peer, time), BF16),
            [pltpu.VMEM((blocks, rows // 2 + 2 * EDGE, LANES), F32)],
        )

    far_out = receivers(1)
    far_in = [swap(far_out[r], r + half_peers, peers) for r in range(half_peers)]
    near_out = receivers(0)
    near_in = [near_out[0]] + [swap(near_out[r], r, peers) for r in range(1, half_peers)]

    tables = [jnp.transpose(v[:, 0], (0, 2, 1)) for v in (src_delay, src_frac)]
    source_tables = call(
        functools.partial(source_tables_kernel, peers, share, calls),
        (source_taper, *tables),
        (
            shape((peers, peers, per_peer, LANES), I32),
            shape((len(calls), peers, 4 * per_peer, len(calls[0]) * share * per_peer), BF16),
        ),
    )
    arrived = near_in + far_in
    result = None
    for turn, groups in enumerate(calls):
        last = turn == len(calls) - 1
        extra = [] if turn == 0 else [result]
        ins = [arrived[g * share + e] for g in groups for e in range(share)]
        scratch = [pltpu.VMEM((len(ins), blocks, per_peer, LANES), F32)]
        if last:
            scratch += [pltpu.VMEM((peers, per_peer, time), BF16), pltpu.SemaphoreType.DMA((peers,))]
        result = call(
            functools.partial(source_kernel, turn, last, peers, share, groups),
            (*source_tables, band, *ins, *extra),
            shape((peers, per_peer, time), BF16) if last else shape((2, peers, per_peer, time), F32),
            scratch,
            out_specs=ANY if last else VMEM,
        )
    return result.reshape(peers, 1, per_peer, time)


def swap(block, step, peers):
    return lax.ppermute(block, "shot", [(i, i ^ step) for i in range(peers)])


def solution(mesh):
    return jax.shard_map(
        body,
        mesh=mesh,
        in_specs=(
            P(("slab", "shot"), "rcv", None),
            P(("slab", "shot"), "rcv", None),
            P(("slab", "shot"), "rcv", None),
            P(("slab", "shot")),
            P("slab", "rcv", "shot", None),
            P("slab", "rcv", "shot", None),
            P(),
            P(),
        ),
        out_specs=P("slab", "rcv", "shot", None),
        check_vma=False,
    )
```

```python
import functools
import math

import jax
import jax.numpy as jnp
from jax import lax
from jax.experimental import pallas as pl
from jax.experimental.pallas import tpu as pltpu
from jax.sharding import PartitionSpec as P


AR = 4
AS = 4
TRI = 2
KR = 9
KS = 9
LANES = 128
SUB = 8
EDGE = 16
PIECES = 4
F32 = jnp.float32
BF16 = jnp.bfloat16
I32 = jnp.int32
GRANT = 24 << 20


def iota(shape, axis):
    return lax.broadcasted_iota(I32, shape, axis)


def filter_band(width):
    size = (3 * LANES, LANES)
    away = jnp.abs(iota(size, 1) - (iota(size, 0) - LANES))
    energy = float(sum((TRI - abs(m)) ** 2 for m in range(1 - TRI, TRI)))
    one = (jnp.maximum(TRI - away, 0).astype(F32) / math.sqrt(energy)).astype(BF16)
    blank = jnp.zeros((LANES, LANES), BF16)
    count = width // LANES
    columns = [jnp.concatenate([blank] * i + [one] + [blank] * (count - 1 - i), axis=0) for i in range(count)]
    return jnp.concatenate(columns, axis=1)


def pair_of(blocks):
    return 2 if blocks % 2 == 0 else 1


def filtered(source, band, store):
    rows, time = source.shape
    high, wide = band.shape
    blank = jnp.zeros((rows, LANES), BF16)
    padded = jnp.concatenate([blank, source, blank], axis=1)
    stack = jnp.concatenate([padded[:, t : t + high] for t in range(0, time, wide)], axis=0)
    dot = jnp.dot(stack, band[...], preferred_element_type=F32).astype(BF16).astype(F32)
    for i, t in enumerate(range(0, time, wide)):
        for j in range(0, wide, LANES):
            store((t + j) // LANES, dot[i * rows : (i + 1) * rows, j : j + LANES])


def filtered_few(source, band):
    rows, time = source.shape
    blank = jnp.zeros((rows, LANES), BF16)
    wide = jnp.concatenate([blank, source, blank], axis=1)
    stack = jnp.concatenate([wide[:, t : t + 3 * LANES] for t in range(0, time, LANES)], axis=0)
    dot = jnp.dot(stack, band[: 3 * LANES, :LANES], preferred_element_type=F32).astype(BF16).astype(F32)
    return [dot[i : i + rows] for i in range(0, dot.shape[0], rows)]


def spread(table, pick):
    dims = (((0,), (0,)), ((), ()))
    return lax.dot_general(table.astype(F32).astype(BF16), pick.astype(BF16), dims, preferred_element_type=F32)


def weight_parts(frac, taper, keep):
    two = jnp.where(keep, frac * (taper * (1.0 / 256.0)), 0.0)
    one = jnp.where(keep, taper, 0.0) - two
    parts = []
    for value in (one, two):
        high = value.astype(BF16).astype(F32)
        parts += [high, value - high]
    return parts


def shifted(load, place, blocks):
    index = place & (LANES - 1)
    here = place < LANES
    moved = [jnp.take_along_axis(load(b), index, axis=1, mode="promise_in_bounds") for b in range(blocks)]
    moved.append(jnp.zeros_like(moved[0]))
    return [jnp.where(here, moved[b], moved[b + 1]) for b in range(blocks)]


def sums(weights, taps, blocks, rows):
    first, second = [], []
    step = pair_of(blocks)
    for b in range(0, blocks, step):
        stack = jnp.concatenate(
            [jnp.concatenate([tap[b + i] for tap in taps], axis=0).astype(BF16) for i in range(step)], axis=1
        )
        dot = jnp.dot(weights, stack, preferred_element_type=F32)
        for i in range(step):
            cols = slice(i * LANES, (i + 1) * LANES)
            first.append(dot[:rows, cols] + dot[rows : 2 * rows, cols])
            second.append(dot[2 * rows : 3 * rows, cols] + dot[3 * rows :, cols])
    return first, second


def products(weights, taps, blocks, rows):
    values = []
    step = pair_of(blocks)
    for b in range(0, blocks, step):
        stack = jnp.concatenate(
            [jnp.concatenate([tap[b + i] for tap in taps], axis=0).astype(BF16) for i in range(step)], axis=1
        )
        dot = jnp.dot(weights, stack, preferred_element_type=F32)
        values += [dot[:rows, i * LANES : (i + 1) * LANES] + dot[rows:, i * LANES : (i + 1) * LANES] for i in range(step)]
    return values


def join(first, second):
    rolled = [pltpu.roll(v, LANES - 1, 1) for v in second] + [jnp.zeros_like(second[0])]
    inner = iota(second[0].shape, 1) < LANES - 1
    return [v + jnp.where(inner, rolled[b], rolled[b + 1]) for b, v in enumerate(first)]


def chosen(taper_ref, tap):
    value = jnp.zeros(tap.shape, F32)
    for a in range(taper_ref.shape[0]):
        value = jnp.where(tap == a, taper_ref[a], value)
    return value


def head_kernel(
    live_ref, taper_in, source_taper_in, delay_in, frac_in, traces_in,
    place_ref, weight_ref, filt_ref, band_ref, source_taper_out, taper_ref, source_taper_ref, delay_ref, frac_ref, traces_ref, sem,
):
    pairs = [(delay_in, delay_ref), (frac_in, frac_ref), (taper_in, taper_ref), (source_taper_in, source_taper_ref)]
    height = traces_in.shape[0] // PIECES
    for i in range(PIECES):
        at = pl.ds(i * height, height)
        pairs.append((traces_in.at[at], traces_ref.at[at]))
    copies = [pltpu.make_async_copy(s, t, sem.at[i]) for i, (s, t) in enumerate(pairs)]
    for copy in copies:
        copy.start()
    band_ref[...] = filter_band(band_ref.shape[1])
    for copy in copies[:4]:
        copy.wait()
    rows = delay_ref.shape[2]
    source_taper_out[...] = chosen(source_taper_ref, iota((SUB, LANES), 1))
    delay, frac = delay_ref[:, 0, :], frac_ref[:, 0, :]
    for a in range(KR):
        pick = iota((KR, LANES), 0) == a
        place_ref[a] = iota((rows, LANES), 1) + spread(delay, pick).astype(I32)
    wide = (rows, LANES)
    tap = iota((KR, LANES), 1) // SUB == iota((KR, LANES), 0)
    row, lane = iota(wide, 0), iota(wide, 1)
    line = row + lax.axis_index("rcv") * rows
    live = jnp.minimum(live_ref[0], rows * lax.axis_size("rcv"))
    source = line + lane // SUB - AR
    keep = (lane % SUB == row % SUB) & (lane < KR * SUB) & (source >= 0) & (source < live)
    place = iota((1, rows), 1) + lax.axis_index("rcv") * rows
    fold = jnp.minimum(place + AR, live - 1) - jnp.maximum(place - AR, 0) + 1
    rest = 1.0 / jnp.sqrt(jnp.maximum(fold, 1).astype(F32))
    scale = jnp.zeros(wide, F32)
    for _ in range(3):
        part = rest.astype(BF16).astype(F32)
        rest = rest - part
        scale = scale + spread(part, iota((1, LANES), 1) >= 0)
    taper = chosen(taper_ref, iota((1, LANES), 1) // SUB) * scale
    for i, part in enumerate(weight_parts(spread(frac, tap), taper, keep)):
        weight_ref[i] = part

    def store(b, value):
        filt_ref[b] = value

    for copy in copies[4:]:
        copy.wait()
    filtered(traces_ref[...], band_ref, store)


def receiver_kernel(far, peers, other_ref, place_ref, weight_ref, filt_ref, band_ref, out_ref, src_ref):
    blocks, rows = filt_ref.shape[:2]
    part = rows // 2
    per_peer = rows // peers
    me = lax.axis_index("shot")
    mine = me // (peers // 2)
    half = (1 - mine) if far else mine
    low = me % (peers // 2)
    base = pl.multiple_of(half * part, part)

    left_at = pl.ds(pl.multiple_of(jnp.maximum(base - EDGE, 0), EDGE), EDGE)
    right_at = pl.ds(pl.multiple_of(jnp.minimum(base + part, rows - EDGE), EDGE), EDGE)
    far_side = pl.multiple_of(jnp.where(half == 0, rows - EDGE, 0), EDGE)
    other = filtered_few(other_ref[pl.ds(far_side, EDGE), :], band_ref)
    for b in range(blocks):
        src_ref[b, :EDGE] = jnp.where(half == 0, other[b], filt_ref[b, left_at, :])
        src_ref[b, EDGE : EDGE + part] = filt_ref[b, pl.ds(base, part), :]
        src_ref[b, EDGE + part :] = jnp.where(half == 1, other[b], filt_ref[b, right_at, :])

    step = max(1, min(2, per_peer // SUB))
    count = part // (step * SUB)
    for c in range(count):
        totals = []
        for g in range(c * step, (c + 1) * step):
            at = pl.ds(pl.multiple_of(base + g * SUB, SUB), SUB)
            taps = []
            for a in range(KR):
                row = EDGE + g * SUB + a - AR
                taps.append(shifted(lambda b: src_ref[b, row : row + SUB, :], place_ref[a, at, :], blocks))
            weights = jnp.concatenate([weight_ref[i, at, : KR * SUB] for i in range(4)], axis=0).astype(BF16)
            totals.append(join(*sums(weights, taps, blocks, SUB)))
        first = c * step * SUB
        height = min(step * SUB, per_peer)
        for s in range(0, step * SUB, height):
            peer = ((first + s) // per_peer) ^ low
            start = (first + s) % per_peer
            for b in range(blocks):
                value = jnp.concatenate([t[b] for t in totals], axis=0).astype(BF16)
                out_ref[peer, start : start + height, b * LANES : (b + 1) * LANES] = value[s : s + height]


def source_tables_kernel(peers, share, calls, taper_ref, delay_ref, frac_ref, place_ref, weight_ref):
    rows = delay_ref.shape[2]
    me = lax.axis_index("shot")
    wide = share * rows
    for k in range(peers):
        for p in range(peers):
            place = iota((rows, LANES), 1)
            if abs(p - k) <= AS:
                place = place + spread(delay_ref[k], iota((KS, LANES), 0) == p - k + AS).astype(I32)
            place_ref[k, p] = place

    def shot_of(groups, lane):
        shot = jnp.zeros_like(lane)
        for i, group in enumerate(groups):
            shot = jnp.where(lane // wide == i, ((me // share) ^ group) * share + (lane % wide) // rows, shot)
        return shot

    for k in range(peers):
        frac = frac_ref[k]
        scale = 1.0 / math.sqrt(min(k + AS, peers - 1) - max(k - AS, 0) + 1)
        row, lane = iota((rows, LANES), 0), iota((rows, LANES), 1)
        for c, groups in enumerate(calls):
            used = len(groups) * wide
            tap = shot_of(groups, lane) - k + AS
            keep = (lane % rows == row) & (tap >= 0) & (tap < KS) & (lane < used)
            index = jnp.clip(shot_of(groups, iota((SUB, LANES), 1)) - k + AS, 0, KS - 1)
            taper = jnp.take_along_axis(taper_ref[...], index, axis=1, mode="promise_in_bounds")[:1]
            column = shot_of(groups, iota((KS, LANES), 1)) - k + AS
            parts = weight_parts(
                spread(frac, column == iota((KS, LANES), 0)), taper * scale, keep
            )
            weight_ref[c, k, :, :used] = jnp.concatenate(parts, axis=0).astype(BF16)[:, :used]


def source_kernel(turn, last, peers, share, groups, place_ref, weight_ref, band_ref, *refs):
    used = len(groups) * share
    ins, refs = refs[:used], refs[used:]
    if turn:
        part_ref, refs = refs[0], refs[1:]
    if last:
        out_ref, src_ref, done_ref, sem = refs
    else:
        out_ref, src_ref = refs
    per_peer, time = ins[0].shape
    blocks = time // LANES
    me = lax.axis_index("shot")
    shots = [((me // share) ^ group) * share + e for group in groups for e in range(share)]
    slots = [i * share + ((me % share) ^ e) for i in range(len(groups)) for e in range(share)]

    def store(b, value):
        for i in range(used):
            src_ref[slots[i], b] = value[i * per_peer : (i + 1) * per_peer]

    filtered(jnp.concatenate([ref[...] for ref in ins], axis=0), band_ref, store)
    rows = min(SUB, per_peer)
    copies = []
    for k in range(peers):
        taps, ahead = [], []
        for i in range(used):
            for r in range(0, per_peer, rows):
                at = slice(r, r + rows)
                place = place_ref[k, shots[i], at, :]
                taps.append(shifted(lambda b: src_ref[i, b, at, :], place, blocks))
                if last:
                    ahead.append(shifted(lambda b: src_ref[i, b, at, :], place + 1, blocks))
        weights = weight_ref[turn, k, :, : used * per_peer]
        if last:
            half = 2 * per_peer
            here = products(weights[:half], taps, blocks, per_peer)
            there = products(weights[half:], ahead, blocks, per_peer)
            for b in range(blocks):
                cols = slice(b * LANES, (b + 1) * LANES)
                done_ref[k, :, cols] = (here[b] + there[b] + part_ref[k, :, cols]).astype(BF16)
            copies.append(pltpu.make_async_copy(done_ref.at[k], out_ref.at[k], sem.at[k]))
            copies[-1].start()
            continue
        pair = sums(weights, taps, blocks, per_peer)
        if turn:
            pair = [
                [v + part_ref[i, k, :, b * LANES : (b + 1) * LANES] for b, v in enumerate(part)]
                for i, part in enumerate(pair)
            ]
            for b, value in enumerate(join(*pair)):
                out_ref[k, :, b * LANES : (b + 1) * LANES] = value
        else:
            for i, part in enumerate(pair):
                for b, value in enumerate(part):
                    out_ref[i, k, :, b * LANES : (b + 1) * LANES] = value
    for copy in copies:
        copy.wait()


VMEM = pl.BlockSpec(memory_space=pltpu.VMEM)
SMEM = pl.BlockSpec(memory_space=pltpu.SMEM)
ANY = pl.BlockSpec(memory_space=pl.ANY)


def stay(value):
    return pltpu.with_memory_space_constraint(value, pltpu.HBM)


def call(kernel, args, outs, scratch=(), in_specs=None, out_specs=None):
    return pl.pallas_call(
        kernel,
        out_shape=outs,
        in_specs=in_specs or [VMEM] * len(args),
        out_specs=out_specs or ([VMEM] * len(outs) if isinstance(outs, tuple) else VMEM),
        scratch_shapes=list(scratch),
        compiler_params=pltpu.CompilerParams(vmem_limit_bytes=GRANT),
    )(*args)


def body(traces, rcv_delay, rcv_frac, live_count, src_delay, src_frac, rcv_taper, src_taper):
    rows, time = traces.shape[1:]
    blocks = time // LANES
    peers = lax.axis_size("shot")
    half_peers = peers // 2
    per_peer = rows // peers
    traces = traces[0]
    other = lax.ppermute(traces, "rcv", [(0, 1), (1, 0)])
    shape = jax.ShapeDtypeStruct
    width = pair_of(blocks) * LANES

    share = 1
    groups = list(range(peers // share))
    cut = half_peers // 2
    early = groups[:cut] + groups[half_peers : half_peers + cut]
    late = groups[half_peers - 1 : half_peers]
    calls = [g for g in (early, [g for g in groups if g not in early + late], late) if g]
    delay, frac = (jnp.transpose(v, (2, 0, 1)) for v in (rcv_delay, rcv_frac))
    place, weight, filt, band, source_taper = call(
        head_kernel,
        [live_count, *(stay(v) for v in (rcv_taper, src_taper, delay, frac, traces))],
        (
            shape((KR, rows, LANES), I32),
            shape((4, rows, LANES), F32),
            shape((blocks, rows, LANES), F32),
            shape((width + 2 * LANES, width), BF16),
            shape((SUB, LANES), F32),
        ),
        [
            pltpu.SMEM(rcv_taper.shape, F32),
            pltpu.SMEM(src_taper.shape, F32),
            pltpu.VMEM(delay.shape, I32),
            pltpu.VMEM(frac.shape, I32),
            pltpu.VMEM(traces.shape, BF16),
            pltpu.SemaphoreType.DMA((4 + PIECES,)),
        ],
        in_specs=[SMEM] + [ANY] * 5,
    )

    def receivers(far):
        return call(
            functools.partial(receiver_kernel, far, peers),
            (other, place, weight, filt, band),
            shape((half_peers, per_peer, time), BF16),
            [pltpu.VMEM((blocks, rows // 2 + 2 * EDGE, LANES), F32)],
        )

    far_out = receivers(1)
    far_in = [swap(far_out[r], r + half_peers, peers) for r in range(half_peers)]
    near_out = receivers(0)
    near_in = [near_out[0]] + [swap(near_out[r], r, peers) for r in range(1, half_peers)]

    tables = [jnp.transpose(v[:, 0], (0, 2, 1)) for v in (src_delay, src_frac)]
    source_tables = call(
        functools.partial(source_tables_kernel, peers, share, calls),
        (source_taper, *tables),
        (
            shape((peers, peers, per_peer, LANES), I32),
            shape((len(calls), peers, 4 * per_peer, len(calls[0]) * share * per_peer), BF16),
        ),
    )
    arrived = near_in + far_in
    result = None
    for turn, groups in enumerate(calls):
        last = turn == len(calls) - 1
        extra = [] if turn == 0 else [result]
        ins = [arrived[g * share + e] for g in groups for e in range(share)]
        scratch = [pltpu.VMEM((len(ins), blocks, per_peer, LANES), F32)]
        if last:
            scratch += [pltpu.VMEM((peers, per_peer, time), BF16), pltpu.SemaphoreType.DMA((peers,))]
        result = call(
            functools.partial(source_kernel, turn, last, peers, share, groups),
            (*source_tables, band, *ins, *extra),
            shape((peers, per_peer, time), BF16 if last else F32) if turn else shape((2, peers, per_peer, time), F32),
            scratch,
            out_specs=ANY if last else VMEM,
        )
    return result.reshape(peers, 1, per_peer, time)


def swap(block, step, peers):
    return lax.ppermute(block, "shot", [(i, i ^ step) for i in range(peers)])


def solution(mesh):
    return jax.shard_map(
        body,
        mesh=mesh,
        in_specs=(
            P(("slab", "shot"), "rcv", None),
            P(("slab", "shot"), "rcv", None),
            P(("slab", "shot"), "rcv", None),
            P(("slab", "shot")),
            P("slab", "rcv", "shot", None),
            P("slab", "rcv", "shot", None),
            P(),
            P(),
        ),
        out_specs=P("slab", "rcv", "shot", None),
        check_vma=False,
    )
```
